512 devices in a mesh: seq: 32 (over y, x, core), head: 16 (over z).
Axes of the slice: x: 4, y: 4, z: 16, core: 2. Of those that a mesh axis runs over, the one named last changes fastest.
Arguments:
- queries: bfloat16 [4096, 2048], P('seq', 'head'), may hold values from -6 to 6
- keys: bfloat16 [4096, 2048], P('seq', 'head'), may hold values from -6 to 6
- values: bfloat16 [4096, 4096], P('seq', 'head'), may hold values from -6 to 6
- gate_code: int32 [4096, 32], P('seq', 'head'), may hold values from 1 to 1000
- beta_code: int32 [4096, 32], P('seq', 'head'), may hold values from 1 to 255
- out_grad: bfloat16 [4096, 2048], P('seq', 'head'), may hold values from -6 to 6
- w_out: bfloat16 [4096, 2048], P('head'), may hold values from -0.09375 to 0.09375
Outputs:
- attn_out: bfloat16 [4096, 4096], P('seq', 'head')
- q_grad: float32 [4096, 2048], P('seq', 'head')
- k_grad: float32 [4096, 2048], P('seq', 'head')
- v_grad: float32 [4096, 4096], P('seq', 'head')
- weight_grad: float32 [4096, 2048], P(('head', 'seq'))
The draws below stay inside these ranges and needn't reach their ends.
All inputs are finite; a program needn't handle non-finite values.
Results may differ from the reference program's by a relative error of at most 0.0029.
Values may be sent and summed in bfloat16 or wider, within the bound.
No kernel may reach another device: no remote copies, remote signals or barrier semaphores. Data moves between devices by JAX's collectives and lax.ppermute only.
A program may use at most 64 MiB of HBM per device.

```python
import jax
import jax.numpy as jnp
from jax import lax

D = 2048
HK = 16
HV = 32
HEAD_DIM = 128
SPAN = 64
TOKENS = 4096


def head_levels(key):
    base = jax.random.fold_in(key, 11)
    levels = jax.random.randint(jax.random.fold_in(base, 1), (HV,), 0, 3)
    chosen = jax.random.randint(jax.random.fold_in(base, 2), (), 0, HV)
    position = jax.random.randint(jax.random.fold_in(base, 3), (), 0, TOKENS)
    return (levels.at[chosen].set(2), chosen, position)


def coded_draw(key, salt, cap_table):
    levels, chosen, position = head_levels(key)
    caps = jnp.array(cap_table, jnp.int32)[levels]
    codes = jax.random.randint(jax.random.fold_in(key, salt), (TOKENS, HV), 1, caps[None, :] + 1)
    codes = codes.at[position, chosen].set(cap_table[2])
    codes = codes.at[(position + 1) % TOKENS, chosen].set(1)
    return codes.astype(jnp.int32)


def draw_gate_code(key, part):
    return coded_draw(key, 21, [4, 100, 1000])


def draw_beta_code(key, part):
    return coded_draw(key, 31, [12, 64, 255])


def steps_of(own_key, shape, cuts, least, largest):
    level, own = 1.0, jax.random.fold_in(own_key, 6)
    for axis_at, shards_of in cuts:
        draws = jnp.exp(jax.random.uniform(jax.random.fold_in(own, axis_at), (shards_of,), jnp.float32, least / len(cuts), largest / len(cuts)))
        level = level * jnp.repeat(draws, shape[axis_at] // shards_of).reshape([-1 if axis == axis_at else 1 for axis in range(len(shape))])
    return level


def scatter_about(rng, dims, deviation, most, cuts=(), held_as=jnp.bfloat16):
    values = deviation * jax.random.normal(rng, dims, jnp.float32)
    if cuts:
        values = values * steps_of(rng, dims, cuts, -0.22, 0.18)
    return jnp.clip(values, -most, most).astype(held_as)


def setup_inputs(seed: int = 0) -> dict:
    key_of = jax.random.split(jax.random.key(seed), 8)
    return {
        "queries": scatter_about(key_of[0], (TOKENS, HK * HEAD_DIM), 1.0, 6.0, ((0, 32), (1, 16))),
        "keys": scatter_about(key_of[1], (TOKENS, HK * HEAD_DIM), 1.0, 6.0, ((0, 32), (1, 16))),
        "values": scatter_about(key_of[2], (TOKENS, HV * HEAD_DIM), 1.0, 6.0, ((0, 32), (1, 16))),
        "gate_code": draw_gate_code(jax.random.fold_in(key_of[7], 71), 0),
        "beta_code": draw_beta_code(jax.random.fold_in(key_of[7], 71), 0),
        "out_grad": scatter_about(key_of[5], (TOKENS, D), 1.0, 6.0, ((0, 32), (1, 16))),
        "w_out": scatter_about(key_of[6], (HV * HEAD_DIM, D), (HV * HEAD_DIM) ** -0.5, 0.09375, ((0, 16),)),
    }


norm_eps = 1e-06
gate_step = 1e-06
beta_steps = 256.0
highest = lax.Precision.HIGHEST

def normalize(block_rows):
    return block_rows * lax.rsqrt(lax.optimization_barrier(jnp.sum(block_rows * block_rows, axis=-1, keepdims=True)) + norm_eps)

def block_masks(block):
    row_ids = lax.broadcasted_iota(jnp.int32, (block, block), 0)
    col_ids = lax.broadcasted_iota(jnp.int32, (block, block), 1)
    return (row_ids > col_ids, row_ids >= col_ids)

def span_pass(query_blocks, key_blocks, value_blocks, decay_blocks, beta_blocks, state):
    strict, inclusive = block_masks(query_blocks.shape[1])

    def advance(state, pieces):
        query_block, key_block, value_block, decay_log, beta_block = pieces
        log_cum = jnp.cumsum(decay_log)
        decay_cum = jnp.exp(log_cum)
        ratio = jnp.exp(log_cum[:, None] - log_cum[None, :]) * beta_block[None, :]
        key_gram = jnp.dot(key_block, key_block.T, precision=highest)
        query_key = jnp.dot(query_block, key_block.T, precision=highest)
        lower_mix = jnp.where(strict, ratio * key_gram, 0.0)
        out_mix = jnp.where(inclusive, ratio * query_key, 0.0)
        right_side = value_block - decay_cum[:, None] * jnp.dot(key_block, state, precision=highest)
        new_values = lax.linalg.triangular_solve(lower_mix, right_side, left_side=True, lower=True, unit_diagonal=True)
        outputs = decay_cum[:, None] * jnp.dot(query_block, state, precision=highest) + jnp.dot(out_mix, new_values, precision=highest)
        weights = beta_block * jnp.exp(log_cum[-1] - log_cum)
        next_state = decay_cum[-1] * state + jnp.dot(key_block.T, weights[:, None] * new_values, precision=highest)
        return (next_state, outputs)
    final_state, outputs = lax.scan(advance, state, (query_blocks, key_blocks, value_blocks, decay_blocks, beta_blocks))
    return (outputs, final_state)

def head_forward(query_head, key_head, value_pair, decay_pair, beta_pair, start_pair):
    length, width = query_head.shape
    blocks = length // SPAN
    query_blocks = (normalize(query_head) * width ** (-0.5)).reshape(blocks, SPAN, width)
    key_blocks = normalize(key_head).reshape(blocks, SPAN, width)

    def single(value_head, decay_head, beta_head, start_state):
        outputs, final_state = span_pass(query_blocks, key_blocks, value_head.reshape(blocks, SPAN, width), decay_head.reshape(blocks, SPAN), beta_head.reshape(blocks, SPAN), start_state)
        return (outputs.reshape(length, width), final_state)
    return jax.vmap(single)(value_pair, decay_pair, beta_pair, start_pair)

def reference(queries, keys, values, gate_code, beta_code, out_grad, w_out):
    width = HEAD_DIM
    group = HV // HK
    query_heads = queries.astype(jnp.float32).reshape(TOKENS, HK, width).transpose(1, 0, 2)
    key_heads = keys.astype(jnp.float32).reshape(TOKENS, HK, width).transpose(1, 0, 2)
    value_heads = values.astype(jnp.float32).reshape(TOKENS, HK, group, width).transpose(1, 2, 0, 3)
    decay_logs = jnp.log1p(-gate_code.astype(jnp.float32) * gate_step).reshape(TOKENS, HK, group).transpose(1, 2, 0)
    betas = (beta_code.astype(jnp.float32) / beta_steps).reshape(TOKENS, HK, group).transpose(1, 2, 0)
    out_cot = jnp.dot(out_grad.astype(jnp.float32), w_out.T.astype(jnp.float32), preferred_element_type=jnp.float32)
    cot_heads = out_cot.reshape(TOKENS, HK, group, width).transpose(1, 2, 0, 3)

    def per_head(pieces):
        query_head, key_head, value_pair, decay_pair, beta_pair, cot_pair = pieces
        start_pair = jnp.zeros((group, width, width), jnp.float32)

        def forward(query_in, key_in, value_in):
            return head_forward(query_in, key_in, value_in, decay_pair, beta_pair, start_pair)[0]
        core_out, pullback = jax.vjp(forward, query_head, key_head, value_pair)
        return (core_out,) + pullback(cot_pair)
    core_out, query_grad, key_grad, value_grad = lax.map(per_head, (query_heads, key_heads, value_heads, decay_logs, betas, cot_heads))
    attn_out = core_out.transpose(2, 0, 1, 3).reshape(TOKENS, HV * width).astype(jnp.bfloat16)
    q_grad = query_grad.transpose(1, 0, 2).reshape(TOKENS, HK * width)
    k_grad = key_grad.transpose(1, 0, 2).reshape(TOKENS, HK * width)
    v_grad = value_grad.transpose(2, 0, 1, 3).reshape(TOKENS, HV * width)
    weight_grad = jnp.dot(attn_out.T.astype(jnp.float32), out_grad.astype(jnp.float32), preferred_element_type=jnp.float32) * TOKENS ** (-0.5)
    return (attn_out, q_grad, k_grad, v_grad, weight_grad)
```

```python
import functools

import jax
import jax.numpy as jnp
from jax import lax
from jax.experimental import pallas as pl
from jax.experimental.pallas import tpu as pltpu
from jax.sharding import PartitionSpec as P

WIDTH = 128
norm_eps = 1e-06
gate_step = 1e-06
beta_steps = 256.0
F32 = jnp.float32
BF16 = jnp.bfloat16
HIGHEST = lax.Precision.HIGHEST


def mm(left, right, left_dim=1, right_dim=0):
    return lax.dot_general(
        left,
        right,
        (((left_dim,), (right_dim,)), ((), ())),
        precision=HIGHEST,
        preferred_element_type=F32,
    )


def mm_bf16(left, right, left_dim=1, right_dim=0):
    return lax.dot_general(
        left, right, (((left_dim,), (right_dim,)), ((), ())), preferred_element_type=F32
    )


def ids(length):
    rows = lax.broadcasted_iota(jnp.int32, (length, length), 0)
    cols = lax.broadcasted_iota(jnp.int32, (length, length), 1)
    return rows, cols


def unit_lower_inverse(lower, rows, cols):
    length = lower.shape[0]
    shift = 1
    pair = jnp.right_shift(rows, 1) == jnp.right_shift(cols, 1)
    inverse = jnp.where(rows == cols, 1.0, jnp.where(pair, -lower, 0.0))
    while (1 << shift) < length:
        wider = jnp.right_shift(rows, shift + 1) == jnp.right_shift(cols, shift + 1)
        inner = jnp.right_shift(rows, shift) == jnp.right_shift(cols, shift)
        off = jnp.where(wider & jnp.logical_not(inner), lower, 0.0)
        inverse = inverse - mm(inverse, mm(off, inverse))
        shift += 1
    return inverse


def inverse_norm(block):
    return lax.rsqrt(jnp.sum(block * block, axis=-1, keepdims=True) + norm_eps)


def prepare_kernel(
    q_ref, k_ref, v_ref, gate_ref, beta_ref,
    send_ref, tmat_ref, mix_ref, ratio_ref, uw_ref, probe_ref, local_ref, cols_ref,
):
    length = q_ref.shape[0]
    group = gate_ref.shape[1]
    dests = send_ref.shape[0]
    share = dests // group
    part = WIDTH // share
    q = q_ref[...].astype(F32)
    k = k_ref[...].astype(F32)
    qn = q * inverse_norm(q) * WIDTH ** (-0.5)
    kn = k * inverse_norm(k)
    rows, cols = ids(length)
    gram = mm(kn, kn, 1, 1)
    query_key = mm(qn, kn, 1, 1)
    tri = jnp.where(rows >= cols, 1.0, 0.0)
    logs = jnp.log1p(-(gate_ref[...].astype(F32) * gate_step))
    betas = beta_ref[...].astype(F32) / beta_steps
    for head in range(group):
        span = slice(head * WIDTH, (head + 1) * WIDTH)
        log_cum = mm(tri, jnp.broadcast_to(logs[:, head : head + 1], (length, length)))
        beta_col = jnp.broadcast_to(betas[:, head : head + 1], (length, length))
        ratio = jnp.exp(log_cum - log_cum.T) * beta_col.T
        ratio = jnp.where(rows >= cols, ratio, 0.0)
        lower = jnp.where(rows > cols, ratio * gram, 0.0)
        mix = ratio * query_key
        inverse = unit_lower_inverse(lower, rows, cols)
        decay = jnp.exp(log_cum)
        value = v_ref[:, span].astype(F32)
        uw = mm(inverse, jnp.concatenate([value, decay * kn], axis=1))
        mixed = mm(mix, uw)
        last = log_cum[length - 1 :, :]
        weight = beta_col * jnp.exp(last - log_cum)
        weighted = weight * kn
        uv, wk = uw[:, :WIDTH], uw[:, WIDTH:]
        transition = jnp.where(rows == cols, jnp.exp(last), 0.0) - mm(weighted, wk, 0, 0)
        state_t = mm(uv, weighted, 0, 0)
        for dest in range(share):
            send_ref[head * share + dest, :WIDTH, :] = transition
            send_ref[head * share + dest, WIDTH:, :] = state_t[dest * part : (dest + 1) * part, :]
        tmat_ref[head] = inverse
        mix_ref[head] = mix
        ratio_ref[head] = ratio
        uw_ref[head] = uw
        probe_ref[head] = decay * qn - mixed[:, WIDTH:]
        local_ref[:, span] = mixed[:, :WIDTH]
        cols_ref[head, 0] = decay
        cols_ref[head, 1] = weight


def cotangent_kernel(grad_ref, w_ref, probe_ref, cot_ref, send_ref):
    blocks = grad_ref.shape[0]
    group = probe_ref.shape[0]
    total = jnp.zeros(cot_ref.shape, F32)
    for block in range(0, blocks, 2):
        left = jnp.concatenate([grad_ref[block], grad_ref[block + 1]], axis=1)
        total += mm_bf16(left, w_ref[:, block * WIDTH : (block + 2) * WIDTH], 1, 1)
    cot_ref[...] = total
    dests, part, _ = send_ref.shape
    share = dests // group
    for head in range(group):
        carried_t = mm(total[:, head * WIDTH : (head + 1) * WIDTH], probe_ref[head], 0, 0)
        send_ref[head * share : (head + 1) * share] = carried_t.reshape(share, part, WIDTH)


def forward_scan_kernel(got_ref, send_ref):
    slabs, part = send_ref.shape[0], send_ref.shape[1]
    state = jnp.zeros((part, WIDTH), F32)
    for slab in range(slabs):
        send_ref[slab] = state
        if slab < slabs - 1:
            state = mm(state, got_ref[slab, :WIDTH, :], 1, 1) + got_ref[slab, WIDTH:, :]


def backward_scan_kernel(got_ref, cot_ref, send_ref):
    slabs, part = send_ref.shape[0], send_ref.shape[1]
    state = jnp.zeros((part, WIDTH), F32)
    for slab in reversed(range(slabs)):
        send_ref[slab] = state
        if slab > 0:
            state = mm(state, got_ref[slab, :WIDTH, :], 1, 0) + cot_ref[slab]


def output_kernel(state_ref, probe_ref, local_ref, grad_ref, attn_ref, send_ref):
    group = probe_ref.shape[0]
    dests, part, _ = send_ref.shape
    share = dests // group
    outs = []
    for head in range(group):
        state_t = state_ref[head * share : (head + 1) * share].reshape(WIDTH, WIDTH)
        outs.append(mm(probe_ref[head], state_t, 1, 1))
    attn = (jnp.concatenate(outs, axis=1) + local_ref[...]).astype(BF16)
    attn_ref[...] = attn
    for block in range(0, grad_ref.shape[0], 2):
        right = jnp.concatenate([grad_ref[block], grad_ref[block + 1]], axis=1)
        term = mm_bf16(attn, right, 0, 0)
        send_ref[:, :, block * WIDTH : (block + 2) * WIDTH] = term.reshape(
            dests, part, 2 * WIDTH
        ).astype(BF16)


def gradient_kernel(
    q_ref, k_ref, state_ref, end_ref, cot_ref, tmat_ref, mix_ref, ratio_ref, uw_ref, cols_ref,
    q_grad_ref, k_grad_ref, v_grad_ref,
):
    length = q_ref.shape[0]
    group = tmat_ref.shape[0]
    share = state_ref.shape[0] // group
    q = q_ref[...].astype(F32)
    k = k_ref[...].astype(F32)
    q_inv = inverse_norm(q)
    k_inv = inverse_norm(k)
    qn = q * q_inv * WIDTH ** (-0.5)
    kn = k * k_inv
    rows, cols = ids(length)
    dq = jnp.zeros((length, WIDTH), F32)
    dk = jnp.zeros((length, WIDTH), F32)
    for head in range(group):
        span = slice(head * WIDTH, (head + 1) * WIDTH)
        state_t = state_ref[head * share : (head + 1) * share].reshape(WIDTH, WIDTH)
        end_t = end_ref[head * share : (head + 1) * share].reshape(WIDTH, WIDTH)
        cot = cot_ref[:, span]
        ratio = ratio_ref[head]
        decay = cols_ref[head, 0]
        weight = cols_ref[head, 1]
        new_values = uw_ref[head, :, :WIDTH] - mm(uw_ref[head, :, WIDTH:], state_t, 1, 1)
        d_new = mm(mix_ref[head], cot, 0, 0) + mm(weight * kn, end_t, 1, 1)
        d_value = mm(tmat_ref[head], d_new, 0, 0)
        v_grad_ref[:, span] = d_value
        d_mix = mm(cot, new_values, 1, 1) * ratio
        d_gram = jnp.where(rows > cols, -mm(d_value, new_values, 1, 1) * ratio, 0.0)
        dq += decay * mm(cot, state_t) + mm(d_mix, kn)
        dk += (
            weight * mm(new_values, end_t)
            - decay * mm(d_value, state_t)
            + mm(d_mix, qn, 0, 0)
            + mm(d_gram + d_gram.T, kn)
        )
    dq = dq * WIDTH ** (-0.5)
    q_grad_ref[...] = q_inv * dq - q * (
        q_inv * q_inv * q_inv * jnp.sum(q * dq, axis=-1, keepdims=True)
    )
    k_grad_ref[...] = k_inv * dk - k * (
        k_inv * k_inv * k_inv * jnp.sum(k * dk, axis=-1, keepdims=True)
    )


def call(kernel, outs, flops, *operands):
    moved = sum(x.size * x.dtype.itemsize for x in operands) + sum(
        x.size * x.dtype.itemsize for x in outs
    )
    return pl.pallas_call(
        kernel,
        out_shape=outs,
        name=kernel.__name__,
        cost_estimate=pl.CostEstimate(flops=flops, bytes_accessed=moved, transcendentals=0),
        compiler_params=pltpu.CompilerParams(vmem_limit_bytes=48 << 20),
    )(*operands)


def shape(dims, dtype=F32):
    return jax.ShapeDtypeStruct(dims, dtype)


def swap(value, axis):
    return lax.all_to_all(value, axis, 0, 0, tiled=True)


def per_device(queries, keys, values, gate_code, beta_code, out_grad, w_out):
    length = queries.shape[0]
    group = values.shape[1] // queries.shape[1]
    slabs = lax.axis_size("seq")
    heads = lax.axis_size("head")
    share = slabs // group
    part = WIDTH // share
    square = (group, length, WIDTH)
    full_grad = swap(jnp.broadcast_to(out_grad[None], (heads, length, WIDTH)), "head")
    send, tmat, mix, ratio, uw, probe, local, columns = call(
        prepare_kernel,
        [
            shape((slabs, WIDTH + part, WIDTH)),
            shape(square),
            shape(square),
            shape(square),
            shape((group, length, 2 * WIDTH)),
            shape(square),
            shape((length, group * WIDTH)),
            shape((group, 2, length, WIDTH)),
        ],
        1 << 30,
        queries, keys, values, gate_code, beta_code,
    )
    got = swap(send, "seq")
    cot, cot_send = call(
        cotangent_kernel,
        [shape((length, group * WIDTH)), shape((slabs, part, WIDTH))],
        1 << 28,
        full_grad, w_out, probe,
    )
    cot_got = swap(cot_send, "seq")
    (start_send,) = call(forward_scan_kernel, [shape((slabs, part, WIDTH))], 1 << 29, got)
    start = swap(start_send, "seq")
    (end_send,) = call(
        backward_scan_kernel, [shape((slabs, part, WIDTH))], 1 << 29, got, cot_got
    )
    end = swap(end_send, "seq")
    attn_out, grad_send = call(
        output_kernel,
        [shape((length, group * WIDTH), BF16), shape((slabs, part, heads * WIDTH), BF16)],
        1 << 28,
        start, probe, local, full_grad,
    )
    grad_got = swap(grad_send, "seq")
    q_grad, k_grad, v_grad = call(
        gradient_kernel,
        [shape((length, WIDTH)), shape((length, WIDTH)), shape((length, group * WIDTH))],
        1 << 29,
        queries, keys, start, end, cot, tmat, mix, ratio, uw, columns,
    )
    scaling = (length * slabs) ** (-0.5)
    weight_grad = jnp.sum(grad_got.astype(F32), axis=0) * scaling
    return (attn_out, q_grad, k_grad, v_grad, weight_grad)


def solution(mesh):
    in_specs = (
        P("seq", "head"),
        P("seq", "head"),
        P("seq", "head"),
        P("seq", "head"),
        P("seq", "head"),
        P("seq", "head"),
        P("head", None),
    )
    out_specs = (
        P("seq", "head"),
        P("seq", "head"),
        P("seq", "head"),
        P("seq", "head"),
        P(("head", "seq"), None),
    )
    return jax.shard_map(
        per_device, mesh=mesh, in_specs=in_specs, out_specs=out_specs, check_vma=False
    )
```

```python
import functools

import jax
import jax.numpy as jnp
from jax import lax
from jax.experimental import pallas as pl
from jax.experimental.pallas import tpu as pltpu
from jax.sharding import PartitionSpec as P

WIDTH = 128
norm_eps = 1e-06
gate_step = 1e-06
beta_steps = 256.0
F32 = jnp.float32
BF16 = jnp.bfloat16
HIGHEST = lax.Precision.HIGHEST


def mm(left, right, left_dim=1, right_dim=0):
    return lax.dot_general(
        left,
        right,
        (((left_dim,), (right_dim,)), ((), ())),
        precision=HIGHEST,
        preferred_element_type=F32,
    )


def mm_bf16(left, right, left_dim=1, right_dim=0):
    return lax.dot_general(
        left, right, (((left_dim,), (right_dim,)), ((), ())), preferred_element_type=F32
    )


def ids(length):
    rows = lax.broadcasted_iota(jnp.int32, (length, length), 0)
    cols = lax.broadcasted_iota(jnp.int32, (length, length), 1)
    return rows, cols


def unit_lower_inverse(lower, rows, cols):
    length = lower.shape[0]
    shift = 1
    pair = jnp.right_shift(rows, 1) == jnp.right_shift(cols, 1)
    inverse = jnp.where(rows == cols, 1.0, jnp.where(pair, -lower, 0.0))
    while (1 << shift) < length:
        wider = jnp.right_shift(rows, shift + 1) == jnp.right_shift(cols, shift + 1)
        inner = jnp.right_shift(rows, shift) == jnp.right_shift(cols, shift)
        off = jnp.where(wider & jnp.logical_not(inner), lower, 0.0)
        inverse = inverse - mm(inverse, mm(off, inverse))
        shift += 1
    return inverse


def inverse_norm(block):
    return lax.rsqrt(jnp.sum(block * block, axis=-1, keepdims=True) + norm_eps)


def split_bf16(value):
    high = value.astype(BF16)
    return high, (value - high.astype(F32)).astype(BF16)


def prepare_kernel(
    q_ref, k_ref, v_ref, gate_ref, beta_ref,
    pair_ref, tmat_ref, mix_ref, ratio_ref, uw_ref, probe_ref, local_ref, cols_ref,
):
    length = q_ref.shape[0]
    group = gate_ref.shape[0]
    q = q_ref[...].astype(F32)
    k = k_ref[...].astype(F32)
    qn = q * inverse_norm(q) * WIDTH ** (-0.5)
    kn = k * inverse_norm(k)
    rows, cols = ids(length)
    gram = mm(kn, kn, 1, 1)
    query_key = mm(qn, kn, 1, 1)
    tri = jnp.where(rows >= cols, 1.0, 0.0)
    logs = jnp.log1p(-(gate_ref[...].astype(F32) * gate_step))
    betas = beta_ref[...].astype(F32) / beta_steps
    for head in range(group):
        span = slice(head * WIDTH, (head + 1) * WIDTH)
        log_cum = mm(tri, jnp.broadcast_to(logs[head : head + 1, :], (length, length)), 1, 1)
        beta_row = jnp.broadcast_to(betas[head : head + 1, :], (length, length))
        ratio = jnp.exp(log_cum - log_cum.T) * beta_row
        ratio = jnp.where(rows >= cols, ratio, 0.0)
        lower = jnp.where(rows > cols, ratio * gram, 0.0)
        mix = ratio * query_key
        inverse = unit_lower_inverse(lower, rows, cols)
        decay = jnp.exp(log_cum)
        value = v_ref[:, span].astype(F32)
        uw = mm(inverse, jnp.concatenate([value, decay * kn], axis=1))
        mixed = mm(mix, uw)
        last = log_cum[length - 1 :, :]
        weight = beta_row.T * jnp.exp(last - log_cum)
        weighted = weight * kn
        uv, wk = uw[:, :WIDTH], uw[:, WIDTH:]
        pair_ref[head] = jnp.where(rows == cols, jnp.exp(last), 0.0) - mm(weighted, wk, 0, 0)
        pair_ref[group + head] = mm(uv, weighted, 0, 0)
        tmat_ref[head] = inverse
        mix_ref[head] = mix
        ratio_ref[head] = ratio
        uw_ref[head] = uw
        probe_ref[head] = decay * qn - mixed[:, WIDTH:]
        local_ref[:, span] = mixed[:, :WIDTH]
        cols_ref[head, 0] = decay
        cols_ref[head, 1] = weight


def compose_kernel(
    odd_ref, own_ref, other_ref, probe_ref, local_ref,
    trans_ref, state_ref, diag_ref, probe_out_ref, local_out_ref,
):
    group = probe_ref.shape[0]
    is_odd = odd_ref[0] == 1
    rows, cols = ids(WIDTH)
    half = WIDTH // 2
    for head in range(group):
        span = slice(head * WIDTH, (head + 1) * WIDTH)
        own, other = own_ref[head], other_ref[head]
        own_state, other_state = own_ref[group + head], other_ref[group + head]
        first = jnp.where(is_odd, other, own)
        second = jnp.where(is_odd, own, other)
        first_state = jnp.where(is_odd, other_state, own_state)
        second_state = jnp.where(is_odd, own_state, other_state)
        transition = mm(second, first)
        state_t = mm(first_state, second, 1, 1) + second_state
        rounded = transition.astype(BF16)
        rest = jnp.where(rows == cols, transition - rounded.astype(F32), 0.0)
        diag_ref[head] = jnp.broadcast_to(
            jnp.sum(rest, axis=0, keepdims=True), (diag_ref.shape[1], WIDTH)
        ).astype(BF16)
        trans_ref[head] = jnp.where(is_odd, transition[half:], transition[:half]).astype(BF16)
        high, low = split_bf16(state_t)
        state_ref[head] = jnp.where(is_odd, low, high)
        probe = probe_ref[head]
        local = local_ref[:, span]
        probe_out_ref[head] = jnp.where(is_odd, mm(probe, other), probe)
        local_out_ref[:, span] = jnp.where(is_odd, local + mm(probe, other_state, 1, 1), local)


def cotangent_kernel(
    grad_ref, w_ref, probe_ref, trans_ref, state_ref, diag_ref, cot_ref, send_ref
):
    blocks = grad_ref.shape[0]
    group = probe_ref.shape[0]
    half = WIDTH // 2
    total = jnp.zeros(cot_ref.shape, F32)
    for block in range(0, blocks, 2):
        left = jnp.concatenate([grad_ref[block], grad_ref[block + 1]], axis=1)
        total += mm_bf16(left, w_ref[:, block * WIDTH : (block + 2) * WIDTH], 1, 1)
    cot_ref[...] = total
    chips = send_ref.shape[0]
    part = WIDTH // chips
    for head in range(group):
        carried_t = mm(total[:, head * WIDTH : (head + 1) * WIDTH], probe_ref[head], 0, 0)
        high = carried_t.astype(BF16).astype(F32)
        low = carried_t - high
        state = state_ref[head].astype(F32)
        diag = diag_ref[head].astype(F32)
        trans = trans_ref[head]
        for chip in range(chips):
            mine = slice(chip * part, (chip + 1) * part)
            send_ref[chip, head, :half, :] = trans
            send_ref[chip, head, half:, :] = jnp.concatenate(
                [state[mine], high[mine], low[mine], diag], axis=0
            ).astype(BF16)


def scan_kernel(got_ref, send_ref):
    chips = got_ref.shape[0]
    half = WIDTH // 2
    part = WIDTH // chips

    def step(state, chip, dim):
        high, low = split_bf16(state)
        both = jnp.concatenate([high.astype(F32), low.astype(F32)], axis=0).astype(BF16)
        trans = jnp.concatenate([got_ref[chip, 0, :half, :], got_ref[chip, 1, :half, :]], axis=0)
        rest = got_ref[chip, 0, half:, :].astype(F32)
        other = got_ref[chip, 1, half:, :].astype(F32)
        product = mm_bf16(both, trans, 1, dim)
        moved = product[:part] + product[part:] + state * rest[3 * part :]
        if dim == 1:
            return moved + rest[:part] + other[:part]
        return moved + (
            (rest[part : 2 * part] + other[part : 2 * part])
            + (rest[2 * part : 3 * part] + other[2 * part : 3 * part])
        )

    ahead = jnp.zeros((part, WIDTH), F32)
    back = jnp.zeros((part, WIDTH), F32)
    for turn in range(chips):
        late = chips - 1 - turn
        for core in range(2):
            send_ref[turn, core, :part, :] = ahead
            send_ref[late, core, part:, :] = back
        if turn < chips - 1:
            ahead = step(ahead, turn, 1)
            back = step(back, late, 0)


def gather_rows(got_ref, head, which):
    chips, _, rows, _ = got_ref.shape
    part = rows // 2
    return got_ref[:, head, which * part : (which + 1) * part, :].reshape(chips * part, WIDTH)


def output_kernel(got_ref, probe_ref, local_ref, grad_ref, attn_ref, send_ref):
    group = probe_ref.shape[0]
    dests, part, _ = send_ref.shape
    outs = [mm(probe_ref[head], gather_rows(got_ref, head, 0), 1, 1) for head in range(group)]
    attn = (jnp.concatenate(outs, axis=1) + local_ref[...]).astype(BF16)
    attn_ref[...] = attn
    for block in range(0, grad_ref.shape[0], 2):
        right = jnp.concatenate([grad_ref[block], grad_ref[block + 1]], axis=1)
        term = mm_bf16(attn, right, 0, 0)
        send_ref[:, :, block * WIDTH : (block + 2) * WIDTH] = term.reshape(
            dests, part, 2 * WIDTH
        ).astype(BF16)


def carried_kernel(cot_ref, probe_ref, carried_ref):
    for head in range(probe_ref.shape[0]):
        carried_ref[head] = mm(
            cot_ref[:, head * WIDTH : (head + 1) * WIDTH], probe_ref[head], 0, 0
        )


def gradient_kernel(
    odd_ref, q_ref, k_ref, got_ref, other_ref, carried_ref, cot_ref, tmat_ref, mix_ref,
    ratio_ref, uw_ref, cols_ref, q_grad_ref, k_grad_ref, v_grad_ref,
):
    length = q_ref.shape[0]
    group = tmat_ref.shape[0]
    is_odd = odd_ref[0] == 1
    q = q_ref[...].astype(F32)
    k = k_ref[...].astype(F32)
    q_inv = inverse_norm(q)
    k_inv = inverse_norm(k)
    qn = q * q_inv * WIDTH ** (-0.5)
    kn = k * k_inv
    rows, cols = ids(length)
    dq = jnp.zeros((length, WIDTH), F32)
    dk = jnp.zeros((length, WIDTH), F32)
    for head in range(group):
        span = slice(head * WIDTH, (head + 1) * WIDTH)
        state_t = gather_rows(got_ref, head, 0)
        end_t = gather_rows(got_ref, head, 1)
        other = other_ref[head]
        through_state = mm(state_t, other, 1, 1) + other_ref[group + head]
        through_end = mm(end_t, other) + carried_ref[head]
        state_t = jnp.where(is_odd, through_state, state_t)
        end_t = jnp.where(is_odd, end_t, through_end)
        cot = cot_ref[:, span]
        ratio = ratio_ref[head]
        decay = cols_ref[head, 0]
        weight = cols_ref[head, 1]
        new_values = uw_ref[head, :, :WIDTH] - mm(uw_ref[head, :, WIDTH:], state_t, 1, 1)
        d_new = mm(mix_ref[head], cot, 0, 0) + mm(weight * kn, end_t, 1, 1)
        d_value = mm(tmat_ref[head], d_new, 0, 0)
        v_grad_ref[:, span] = d_value
        d_mix = mm(cot, new_values, 1, 1) * ratio
        d_gram = jnp.where(rows > cols, -mm(d_value, new_values, 1, 1) * ratio, 0.0)
        dq += decay * mm(cot, state_t) + mm(d_mix, kn)
        dk += (
            weight * mm(new_values, end_t)
            - decay * mm(d_value, state_t)
            + mm(d_mix, qn, 0, 0)
            + mm(d_gram + d_gram.T, kn)
        )
    dq = dq * WIDTH ** (-0.5)
    q_grad_ref[...] = q_inv * dq - q * (
        q_inv * q_inv * q_inv * jnp.sum(q * dq, axis=-1, keepdims=True)
    )
    k_grad_ref[...] = k_inv * dk - k * (
        k_inv * k_inv * k_inv * jnp.sum(k * dk, axis=-1, keepdims=True)
    )


def call(kernel, outs, flops, *operands):
    moved = sum(x.size * x.dtype.itemsize for x in operands) + sum(
        x.size * x.dtype.itemsize for x in outs
    )
    scalars = [x.ndim == 1 for x in operands]
    vmem = pl.BlockSpec(memory_space=pltpu.VMEM)
    smem = pl.BlockSpec(memory_space=pltpu.SMEM)
    return pl.pallas_call(
        kernel,
        out_shape=outs,
        in_specs=[smem if scalar else vmem for scalar in scalars],
        out_specs=[vmem] * len(outs),
        name=kernel.__name__,
        cost_estimate=pl.CostEstimate(flops=flops, bytes_accessed=moved, transcendentals=0),
        compiler_params=pltpu.CompilerParams(vmem_limit_bytes=48 << 20),
    )(*operands)


def shape(dims, dtype=F32):
    return jax.ShapeDtypeStruct(dims, dtype)


def swap(value, axis):
    return lax.all_to_all(value, axis, 0, 0, tiled=True)


def per_device(queries, keys, values, gate_code, beta_code, out_grad, w_out):
    length = queries.shape[0]
    group = values.shape[1] // queries.shape[1]
    slabs = lax.axis_size("seq")
    heads = lax.axis_size("head")
    chips = slabs // 2
    part = WIDTH // chips
    square = (group, length, WIDTH)
    flat = (length, group * WIDTH)
    odd = (lax.axis_index("seq") % 2).astype(jnp.int32).reshape(1)
    full_grad = swap(jnp.broadcast_to(out_grad[None], (heads, length, WIDTH)), "head")
    pair, tmat, mix, ratio, uw, probe, local, columns = call(
        prepare_kernel,
        [
            shape((2 * group, WIDTH, WIDTH)),
            shape(square),
            shape(square),
            shape(square),
            shape((group, length, 2 * WIDTH)),
            shape(square),
            shape(flat),
            shape((group, 2, length, WIDTH)),
        ],
        1 << 30,
        queries, keys, values, gate_code.T, beta_code.T,
    )
    other = lax.ppermute(pair, "seq", [(slab, slab ^ 1) for slab in range(slabs)])
    trans, state, diag, chip_probe, chip_local = call(
        compose_kernel,
        [
            shape((group, WIDTH // 2, WIDTH), BF16),
            shape((group, WIDTH, WIDTH), BF16),
            shape((group, part, WIDTH), BF16),
            shape(square),
            shape(flat),
        ],
        1 << 28,
        odd, pair, other, probe, local,
    )
    cot, send = call(
        cotangent_kernel,
        [shape(flat), shape((chips, group, WIDTH // 2 + 4 * part, WIDTH), BF16)],
        1 << 28,
        full_grad, w_out, chip_probe, trans, state, diag,
    )
    got = swap(send.reshape((slabs,) + send.shape[2:]), "seq")
    (carried,) = call(carried_kernel, [shape((group, WIDTH, WIDTH))], 1 << 26, cot, probe)
    carried = lax.ppermute(carried, "seq", [(slab, slab ^ 1) for slab in range(slabs)])
    (back,) = call(
        scan_kernel, [shape((chips, 2, 2 * part, WIDTH))], 1 << 27, got.reshape(send.shape)
    )
    states = swap(back.reshape(slabs, 2 * part, WIDTH), "seq").reshape(back.shape)
    attn_out, grad_send = call(
        output_kernel,
        [shape(flat, BF16), shape((slabs, part, heads * WIDTH), BF16)],
        1 << 28,
        states, chip_probe, chip_local, full_grad,
    )
    grad_got = swap(grad_send, "seq")
    q_grad, k_grad, v_grad = call(
        gradient_kernel,
        [shape((length, WIDTH)), shape((length, WIDTH)), shape(flat)],
        1 << 29,
        odd, queries, keys, states, other, carried, cot, tmat, mix, ratio, uw, columns,
    )
    scaling = (length * slabs) ** (-0.5)
    weight_grad = jnp.sum(grad_got.astype(F32), axis=0) * scaling
    return (attn_out, q_grad, k_grad, v_grad, weight_grad)


def solution(mesh):
    in_specs = (
        P("seq", "head"),
        P("seq", "head"),
        P("seq", "head"),
        P("seq", "head"),
        P("seq", "head"),
        P("seq", "head"),
        P("head", None),
    )
    out_specs = (
        P("seq", "head"),
        P("seq", "head"),
        P("seq", "head"),
        P("seq", "head"),
        P(("head", "seq"), None),
    )
    return jax.shard_map(
        per_device, mesh=mesh, in_specs=in_specs, out_specs=out_specs, check_vma=False
    )
```

```python
import functools

import jax
import jax.numpy as jnp
from jax import lax
from jax.experimental import pallas as pl
from jax.experimental.pallas import tpu as pltpu
from jax.sharding import PartitionSpec as P

WIDTH = 128
norm_eps = 1e-06
gate_step = 1e-06
beta_steps = 256.0
F32 = jnp.float32
BF16 = jnp.bfloat16
HIGHEST = lax.Precision.HIGHEST


def mm(left, right, left_dim=1, right_dim=0):
    return lax.dot_general(
        left,
        right,
        (((left_dim,), (right_dim,)), ((), ())),
        precision=HIGHEST,
        preferred_element_type=F32,
    )


def mm_bf16(left, right, left_dim=1, right_dim=0):
    return lax.dot_general(
        left, right, (((left_dim,), (right_dim,)), ((), ())), preferred_element_type=F32
    )


def ids(length):
    rows = lax.broadcasted_iota(jnp.int32, (length, length), 0)
    cols = lax.broadcasted_iota(jnp.int32, (length, length), 1)
    return rows, cols


def unit_lower_inverse(lower, rows, cols):
    length = lower.shape[0]
    shift = 1
    pair = jnp.right_shift(rows, 1) == jnp.right_shift(cols, 1)
    inverse = jnp.where(rows == cols, 1.0, jnp.where(pair, -lower, 0.0))
    while (1 << shift) < length:
        wider = jnp.right_shift(rows, shift + 1) == jnp.right_shift(cols, shift + 1)
        inner = jnp.right_shift(rows, shift) == jnp.right_shift(cols, shift)
        off = jnp.where(wider & jnp.logical_not(inner), lower, 0.0)
        inverse = inverse - mm(inverse, mm(off, inverse))
        shift += 1
    return inverse


def inverse_norm(block):
    return lax.rsqrt(jnp.sum(block * block, axis=-1, keepdims=True) + norm_eps)


def split_bf16(value):
    high = value.astype(BF16)
    return high, (value - high.astype(F32)).astype(BF16)


def prepare_kernel(
    q_ref, k_ref, v_ref, gate_ref, beta_ref,
    pair_ref, tmat_ref, mix_ref, ratio_ref, uw_ref, probe_ref, local_ref, cols_ref,
):
    length = q_ref.shape[0]
    group = gate_ref.shape[0]
    q = q_ref[...].astype(F32)
    k = k_ref[...].astype(F32)
    qn = q * inverse_norm(q) * WIDTH ** (-0.5)
    kn = k * inverse_norm(k)
    rows, cols = ids(length)
    gram = mm(kn, kn, 1, 1)
    query_key = mm(qn, kn, 1, 1)
    tri = jnp.where(rows >= cols, 1.0, 0.0)
    logs = jnp.log1p(-(gate_ref[...].astype(F32) * gate_step))
    betas = beta_ref[...].astype(F32) / beta_steps
    for head in range(group):
        span = slice(head * WIDTH, (head + 1) * WIDTH)
        log_cum = mm(tri, jnp.broadcast_to(logs[head : head + 1, :], (length, length)), 1, 1)
        beta_row = jnp.broadcast_to(betas[head : head + 1, :], (length, length))
        ratio = jnp.exp(log_cum - log_cum.T) * beta_row
        ratio = jnp.where(rows >= cols, ratio, 0.0)
        lower = jnp.where(rows > cols, ratio * gram, 0.0)
        mix = ratio * query_key
        inverse = unit_lower_inverse(lower, rows, cols)
        decay = jnp.exp(log_cum)
        value = v_ref[:, span].astype(F32)
        uw = mm(inverse, jnp.concatenate([value, decay * kn], axis=1))
        mixed = mm(mix, uw)
        last = log_cum[length - 1 :, :]
        weight = beta_row.T * jnp.exp(last - log_cum)
        weighted = weight * kn
        uv, wk = uw[:, :WIDTH], uw[:, WIDTH:]
        pair_ref[head] = jnp.where(rows == cols, jnp.exp(last), 0.0) - mm(weighted, wk, 0, 0)
        pair_ref[group + head] = mm(uv, weighted, 0, 0)
        tmat_ref[head] = inverse
        mix_ref[head] = mix
        ratio_ref[head] = ratio
        uw_ref[head] = uw
        probe_ref[head] = decay * qn - mixed[:, WIDTH:]
        local_ref[:, span] = mixed[:, :WIDTH]
        cols_ref[head, 0] = decay
        cols_ref[head, 1] = weight


def compose_kernel(
    odd_ref, own_ref, other_ref, probe_ref, local_ref,
    trans_ref, state_ref, diag_ref, maps_ref,
):
    group = probe_ref.shape[0]
    is_odd = odd_ref[0] == 1
    rows, cols = ids(WIDTH)
    half = WIDTH // 2
    for head in range(group):
        span = slice(head * WIDTH, (head + 1) * WIDTH)
        own, other = own_ref[head], other_ref[head]
        own_state, other_state = own_ref[group + head], other_ref[group + head]
        first = jnp.where(is_odd, other, own)
        second = jnp.where(is_odd, own, other)
        first_state = jnp.where(is_odd, other_state, own_state)
        second_state = jnp.where(is_odd, own_state, other_state)
        transition = mm(second, first)
        state_t = mm(first_state, second, 1, 1) + second_state
        rounded = transition.astype(BF16)
        rest = jnp.where(rows == cols, transition - rounded.astype(F32), 0.0)
        diag_ref[head] = jnp.broadcast_to(
            jnp.sum(rest, axis=0, keepdims=True), (diag_ref.shape[1], WIDTH)
        ).astype(BF16)
        trans_ref[head] = jnp.where(is_odd, transition[half:], transition[:half]).astype(BF16)
        high, low = split_bf16(state_t)
        state_ref[head] = jnp.where(is_odd, low, high)
        probe = probe_ref[head]
        local = local_ref[:, span]
        maps_ref[head] = jnp.where(is_odd, mm(probe, other), probe)
        maps_ref[group + head] = jnp.where(is_odd, local + mm(probe, other_state, 1, 1), local)


def cotangent_kernel(
    grad_ref, w_ref, maps_ref, trans_ref, state_ref, diag_ref, cot_ref, send_ref
):
    blocks = grad_ref.shape[0]
    group = trans_ref.shape[0]
    half = WIDTH // 2
    total = jnp.zeros(cot_ref.shape, F32)
    for block in range(0, blocks, 2):
        left = jnp.concatenate([grad_ref[block], grad_ref[block + 1]], axis=1)
        total += mm_bf16(left, w_ref[:, block * WIDTH : (block + 2) * WIDTH], 1, 1)
    cot_ref[...] = total
    chips = send_ref.shape[0]
    part = WIDTH // chips
    for head in range(group):
        carried_t = mm(total[:, head * WIDTH : (head + 1) * WIDTH], maps_ref[head], 0, 0)
        high = carried_t.astype(BF16).astype(F32)
        low = carried_t - high
        state = state_ref[head].astype(F32)
        diag = diag_ref[head].astype(F32)
        trans = trans_ref[head]
        for chip in range(chips):
            mine = slice(chip * part, (chip + 1) * part)
            send_ref[chip, head, :half, :] = trans
            send_ref[chip, head, half:, :] = jnp.concatenate(
                [state[mine], high[mine], low[mine], diag], axis=0
            ).astype(BF16)


def scan_kernel(got_ref, send_ref):
    chips = got_ref.shape[0]
    half = WIDTH // 2
    part = WIDTH // chips

    def step(state, chip, dim):
        high, low = split_bf16(state)
        both = jnp.concatenate([high.astype(F32), low.astype(F32)], axis=0).astype(BF16)
        trans = jnp.concatenate([got_ref[chip, 0, :half, :], got_ref[chip, 1, :half, :]], axis=0)
        rest = got_ref[chip, 0, half:, :].astype(F32)
        other = got_ref[chip, 1, half:, :].astype(F32)
        product = mm_bf16(both, trans, 1, dim)
        moved = product[:part] + product[part:] + state * rest[3 * part :]
        if dim == 1:
            return moved + rest[:part] + other[:part]
        return moved + (
            (rest[part : 2 * part] + other[part : 2 * part])
            + (rest[2 * part : 3 * part] + other[2 * part : 3 * part])
        )

    ahead = jnp.zeros((part, WIDTH), F32)
    back = jnp.zeros((part, WIDTH), F32)
    for turn in range(chips):
        late = chips - 1 - turn
        for core in range(2):
            send_ref[turn, core, :part, :] = ahead
            send_ref[late, core, part:, :] = back
        if turn < chips - 1:
            ahead = step(ahead, turn, 1)
            back = step(back, late, 0)


def gather_rows(got_ref, head, which):
    chips, _, rows, _ = got_ref.shape
    part = rows // 2
    return got_ref[:, head, which * part : (which + 1) * part, :].reshape(chips * part, WIDTH)


def output_kernel(
    odd_ref, got_ref, maps_ref, other_maps_ref, grad_ref, other_grad_ref, attn_ref, send_ref
):
    group = maps_ref.shape[0] // 2
    dests, part, _ = send_ref.shape
    blocks = other_grad_ref.shape[0]
    first = odd_ref[0] * blocks
    own, other = [], []
    for head in range(group):
        state_t = gather_rows(got_ref, head, 0)
        own.append(mm(maps_ref[head], state_t, 1, 1) + maps_ref[group + head])
        other.append(mm(other_maps_ref[head], state_t, 1, 1) + other_maps_ref[group + head])
    own = jnp.concatenate(own, axis=1).astype(BF16)
    other = jnp.concatenate(other, axis=1).astype(BF16)
    attn_ref[...] = own
    left = jnp.concatenate([own, other], axis=0)
    for block in range(0, blocks, 2):
        right = jnp.concatenate(
            [
                jnp.concatenate([grad_ref[first + block], grad_ref[first + block + 1]], axis=1),
                jnp.concatenate([other_grad_ref[block], other_grad_ref[block + 1]], axis=1),
            ],
            axis=0,
        )
        term = mm_bf16(left, right, 0, 0)
        send_ref[:, :, block * WIDTH : (block + 2) * WIDTH] = term.reshape(
            dests, part, 2 * WIDTH
        ).astype(BF16)


def sum_kernel(got_ref, out_ref, *, scaling):
    chips, cores, _, width = got_ref.shape
    for core in range(cores):
        total = got_ref[0, core].astype(F32)
        for chip in range(1, chips):
            total = total + got_ref[chip, core].astype(F32)
        out_ref[:, core * width : (core + 1) * width] = total * scaling


def half_kernel(odd_ref, grad_ref, half_ref):
    blocks = half_ref.shape[0]
    half_ref[...] = grad_ref[pl.ds((1 - odd_ref[0]) * blocks, blocks)]


def carried_kernel(cot_ref, probe_ref, carried_ref):
    for head in range(probe_ref.shape[0]):
        carried_ref[head] = mm(
            cot_ref[:, head * WIDTH : (head + 1) * WIDTH], probe_ref[head], 0, 0
        )


def gradient_kernel(
    odd_ref, q_ref, k_ref, got_ref, other_ref, carried_ref, cot_ref, tmat_ref, mix_ref,
    ratio_ref, uw_ref, cols_ref, q_grad_ref, k_grad_ref, v_grad_ref,
):
    length = q_ref.shape[0]
    group = tmat_ref.shape[0]
    is_odd = odd_ref[0] == 1
    q = q_ref[...].astype(F32)
    k = k_ref[...].astype(F32)
    q_inv = inverse_norm(q)
    k_inv = inverse_norm(k)
    qn = q * q_inv * WIDTH ** (-0.5)
    kn = k * k_inv
    rows, cols = ids(length)
    dq = jnp.zeros((length, WIDTH), F32)
    dk = jnp.zeros((length, WIDTH), F32)
    for head in range(group):
        span = slice(head * WIDTH, (head + 1) * WIDTH)
        state_t = gather_rows(got_ref, head, 0)
        end_t = gather_rows(got_ref, head, 1)
        other = other_ref[head]
        through_state = mm(state_t, other, 1, 1) + other_ref[group + head]
        through_end = mm(end_t, other) + carried_ref[head]
        state_t = jnp.where(is_odd, through_state, state_t)
        end_t = jnp.where(is_odd, end_t, through_end)
        cot = cot_ref[:, span]
        ratio = ratio_ref[head]
        decay = cols_ref[head, 0]
        weight = cols_ref[head, 1]
        new_values = uw_ref[head, :, :WIDTH] - mm(uw_ref[head, :, WIDTH:], state_t, 1, 1)
        d_new = mm(mix_ref[head], cot, 0, 0) + mm(weight * kn, end_t, 1, 1)
        d_value = mm(tmat_ref[head], d_new, 0, 0)
        v_grad_ref[:, span] = d_value
        d_mix = mm(cot, new_values, 1, 1) * ratio
        d_gram = jnp.where(rows > cols, -mm(d_value, new_values, 1, 1) * ratio, 0.0)
        dq += decay * mm(cot, state_t) + mm(d_mix, kn)
        dk += (
            weight * mm(new_values, end_t)
            - decay * mm(d_value, state_t)
            + mm(d_mix, qn, 0, 0)
            + mm(d_gram + d_gram.T, kn)
        )
    dq = dq * WIDTH ** (-0.5)
    q_grad_ref[...] = q_inv * dq - q * (
        q_inv * q_inv * q_inv * jnp.sum(q * dq, axis=-1, keepdims=True)
    )
    k_grad_ref[...] = k_inv * dk - k * (
        k_inv * k_inv * k_inv * jnp.sum(k * dk, axis=-1, keepdims=True)
    )


def call(kernel, outs, flops, *operands):
    moved = sum(x.size * x.dtype.itemsize for x in operands) + sum(
        x.size * x.dtype.itemsize for x in outs
    )
    scalars = [x.ndim == 1 for x in operands]
    vmem = pl.BlockSpec(memory_space=pltpu.VMEM)
    smem = pl.BlockSpec(memory_space=pltpu.SMEM)
    return pl.pallas_call(
        kernel,
        out_shape=outs,
        in_specs=[smem if scalar else vmem for scalar in scalars],
        out_specs=[vmem] * len(outs),
        name=getattr(kernel, "func", kernel).__name__,
        cost_estimate=pl.CostEstimate(flops=flops, bytes_accessed=moved, transcendentals=0),
        compiler_params=pltpu.CompilerParams(vmem_limit_bytes=48 << 20),
    )(*operands)


def shape(dims, dtype=F32):
    return jax.ShapeDtypeStruct(dims, dtype)


def swap(value, axis):
    return lax.all_to_all(value, axis, 0, 0, tiled=True)


def across(value):
    slabs = lax.axis_size("seq")
    return lax.ppermute(value, "seq", [(slab, slab ^ 1) for slab in range(slabs)])


def per_device(queries, keys, values, gate_code, beta_code, out_grad, w_out):
    length = queries.shape[0]
    group = values.shape[1] // queries.shape[1]
    slabs = lax.axis_size("seq")
    heads = lax.axis_size("head")
    chips = slabs // 2
    part = WIDTH // chips
    square = (group, length, WIDTH)
    flat = (length, group * WIDTH)
    odd = (lax.axis_index("seq") % 2).astype(jnp.int32).reshape(1)
    full_grad = swap(jnp.broadcast_to(out_grad[None], (heads, length, WIDTH)), "head")
    pair, tmat, mix, ratio, uw, probe, local, columns = call(
        prepare_kernel,
        [
            shape((2 * group, WIDTH, WIDTH)),
            shape(square),
            shape(square),
            shape(square),
            shape((group, length, 2 * WIDTH)),
            shape(square),
            shape(flat),
            shape((group, 2, length, WIDTH)),
        ],
        1 << 30,
        queries, keys, values, gate_code.T, beta_code.T,
    )
    other = across(pair)
    trans, state, diag, maps = call(
        compose_kernel,
        [
            shape((group, WIDTH // 2, WIDTH), BF16),
            shape((group, WIDTH, WIDTH), BF16),
            shape((group, part, WIDTH), BF16),
            shape((2 * group, length, WIDTH)),
        ],
        1 << 28,
        odd, pair, other, probe, local,
    )
    other_maps = across(maps)
    cot, send = call(
        cotangent_kernel,
        [shape(flat), shape((chips, group, WIDTH // 2 + 4 * part, WIDTH), BF16)],
        1 << 28,
        full_grad, w_out, maps, trans, state, diag,
    )
    (half,) = call(
        half_kernel, [shape((heads // 2, length, WIDTH), BF16)], 1 << 20, odd, full_grad
    )
    other_half = across(half)
    got = swap(send.reshape((slabs,) + send.shape[2:]), "seq")
    (carried,) = call(carried_kernel, [shape((group, WIDTH, WIDTH))], 1 << 26, cot, probe)
    carried = across(carried)
    (back,) = call(
        scan_kernel, [shape((chips, 2, 2 * part, WIDTH))], 1 << 27, got.reshape(send.shape)
    )
    states = swap(back.reshape(slabs, 2 * part, WIDTH), "seq").reshape(back.shape)
    attn_out, grad_send = call(
        output_kernel,
        [shape(flat, BF16), shape((slabs, part, heads // 2 * WIDTH), BF16)],
        1 << 28,
        odd, states, maps, other_maps, full_grad, other_half,
    )
    grad_got = swap(grad_send, "seq")
    q_grad, k_grad, v_grad = call(
        gradient_kernel,
        [shape((length, WIDTH)), shape((length, WIDTH)), shape(flat)],
        1 << 29,
        odd, queries, keys, states, other, carried, cot, tmat, mix, ratio, uw, columns,
    )
    scaling = (length * slabs) ** (-0.5)
    (weight_grad,) = call(
        functools.partial(sum_kernel, scaling=scaling),
        [shape((part, heads * WIDTH))],
        1 << 20,
        grad_got.reshape((chips, 2) + grad_got.shape[1:]),
    )
    return (attn_out, q_grad, k_grad, v_grad, weight_grad)


def solution(mesh):
    in_specs = (
        P("seq", "head"),
        P("seq", "head"),
        P("seq", "head"),
        P("seq", "head"),
        P("seq", "head"),
        P("seq", "head"),
        P("head", None),
    )
    out_specs = (
        P("seq", "head"),
        P("seq", "head"),
        P("seq", "head"),
        P("seq", "head"),
        P(("head", "seq"), None),
    )
    return jax.shard_map(
        per_device, mesh=mesh, in_specs=in_specs, out_specs=out_specs, check_vma=False
    )
```

```python
import functools

import jax
import jax.numpy as jnp
from jax import lax
from jax.experimental import pallas as pl
from jax.experimental.pallas import tpu as pltpu
from jax.sharding import PartitionSpec as P

WIDTH = 128
norm_eps = 1e-06
gate_step = 1e-06
beta_steps = 256.0
F32 = jnp.float32
BF16 = jnp.bfloat16
HIGHEST = lax.Precision.HIGHEST


def mm(left, right, left_dim=1, right_dim=0):
    return lax.dot_general(
        left,
        right,
        (((left_dim,), (right_dim,)), ((), ())),
        precision=HIGHEST,
        preferred_element_type=F32,
    )


def mm_bf16(left, right, left_dim=1, right_dim=0):
    return lax.dot_general(
        left, right, (((left_dim,), (right_dim,)), ((), ())), preferred_element_type=F32
    )


def ids(length):
    rows = lax.broadcasted_iota(jnp.int32, (length, length), 0)
    cols = lax.broadcasted_iota(jnp.int32, (length, length), 1)
    return rows, cols


def unit_lower_inverse(lower, rows, cols):
    length = lower.shape[0]
    shift = 1
    pair = jnp.right_shift(rows, 1) == jnp.right_shift(cols, 1)
    inverse = jnp.where(rows == cols, 1.0, jnp.where(pair, -lower, 0.0))
    while (1 << shift) < length:
        wider = jnp.right_shift(rows, shift + 1) == jnp.right_shift(cols, shift + 1)
        inner = jnp.right_shift(rows, shift) == jnp.right_shift(cols, shift)
        off = jnp.where(wider & jnp.logical_not(inner), lower, 0.0)
        inverse = inverse - mm(inverse, mm(off, inverse))
        shift += 1
    return inverse


def inverse_norm(block):
    return lax.rsqrt(jnp.sum(block * block, axis=-1, keepdims=True) + norm_eps)


def split_bf16(value):
    high = value.astype(BF16)
    return high, (value - high.astype(F32)).astype(BF16)


def prepare_kernel(
    q_ref, k_ref, v_ref, gate_ref, beta_ref,
    pair_ref, tmat_ref, mix_ref, ratio_ref, uw_ref, probe_ref, local_ref, cols_ref,
):
    length = q_ref.shape[0]
    group = gate_ref.shape[0]
    q = q_ref[...].astype(F32)
    k = k_ref[...].astype(F32)
    qn = q * inverse_norm(q) * WIDTH ** (-0.5)
    kn = k * inverse_norm(k)
    rows, cols = ids(length)
    gram = mm(kn, kn, 1, 1)
    query_key = mm(qn, kn, 1, 1)
    tri = jnp.where(rows >= cols, 1.0, 0.0)
    logs = jnp.log1p(-(gate_ref[...].astype(F32) * gate_step))
    betas = beta_ref[...].astype(F32) / beta_steps
    for head in range(group):
        span = slice(head * WIDTH, (head + 1) * WIDTH)
        log_cum = mm(tri, jnp.broadcast_to(logs[head : head + 1, :], (length, length)), 1, 1)
        beta_row = jnp.broadcast_to(betas[head : head + 1, :], (length, length))
        ratio = jnp.exp(log_cum - log_cum.T) * beta_row
        ratio = jnp.where(rows >= cols, ratio, 0.0)
        lower = jnp.where(rows > cols, ratio * gram, 0.0)
        mix = ratio * query_key
        inverse = unit_lower_inverse(lower, rows, cols)
        decay = jnp.exp(log_cum)
        value = v_ref[:, span].astype(F32)
        uw = mm(inverse, jnp.concatenate([value, decay * kn], axis=1))
        mixed = mm(mix, uw)
        last = log_cum[length - 1 :, :]
        weight = beta_row.T * jnp.exp(last - log_cum)
        weighted = weight * kn
        uv, wk = uw[:, :WIDTH], uw[:, WIDTH:]
        pair_ref[head] = jnp.where(rows == cols, jnp.exp(last), 0.0) - mm(weighted, wk, 0, 0)
        pair_ref[group + head] = mm(uv, weighted, 0, 0)
        tmat_ref[head] = inverse
        mix_ref[head] = mix
        ratio_ref[head] = ratio
        uw_ref[head] = uw
        probe_ref[head] = decay * qn - mixed[:, WIDTH:]
        local_ref[:, span] = mixed[:, :WIDTH]
        cols_ref[head, 0] = decay
        cols_ref[head, 1] = weight


def in_order(late, own, other):
    return jnp.where(late, other, own), jnp.where(late, own, other)


def compose_heads(late, own_ref, other_ref, head, group):
    own, other = own_ref[head], other_ref[head]
    first, second = in_order(late, own, other)
    first_state, second_state = in_order(late, own_ref[group + head], other_ref[group + head])
    return mm(second, first), mm(first_state, second, 1, 1) + second_state


def compose_maps(late, other_ref, head, group, probe, local):
    moved = jnp.where(late, mm(probe, other_ref[head]), probe)
    return moved, jnp.where(late, local + mm(probe, other_ref[group + head], 1, 1), local)


def chip_kernel(flags_ref, own_ref, other_ref, probe_ref, local_ref, chip_ref, maps_ref):
    group = probe_ref.shape[0]
    late = flags_ref[0] == 1
    for head in range(group):
        span = slice(head * WIDTH, (head + 1) * WIDTH)
        chip_ref[head], chip_ref[group + head] = compose_heads(
            late, own_ref, other_ref, head, group
        )
        maps_ref[head], maps_ref[group + head] = compose_maps(
            late, other_ref, head, group, probe_ref[head], local_ref[:, span]
        )


def quad_kernel(
    flags_ref, own_ref, other_ref, chip_maps_ref, trans_ref, state_ref, diag_ref, maps_ref
):
    group = trans_ref.shape[0]
    core = flags_ref[0] == 1
    late = flags_ref[1] == 1
    rows, cols = ids(WIDTH)
    share = WIDTH // 4
    for head in range(group):
        transition, state_t = compose_heads(late, own_ref, other_ref, head, group)
        rounded = transition.astype(BF16)
        rest = jnp.where(rows == cols, transition - rounded.astype(F32), 0.0)
        diag_ref[head] = jnp.broadcast_to(
            jnp.sum(rest, axis=0, keepdims=True), (diag_ref.shape[1], WIDTH)
        ).astype(BF16)
        quarters = [transition[at * share : (at + 1) * share] for at in range(4)]
        trans_ref[head] = jnp.where(
            late,
            jnp.where(core, quarters[3], quarters[2]),
            jnp.where(core, quarters[1], quarters[0]),
        ).astype(BF16)
        high = state_t.astype(BF16).astype(F32)
        part = jnp.where(core, state_t - high, high)
        state_ref[head] = jnp.where(late, 0.0, part).astype(BF16)
        maps_ref[head], maps_ref[group + head] = compose_maps(
            late, other_ref, head, group, chip_maps_ref[head], chip_maps_ref[group + head]
        )


def cotangent_kernel(
    grad_ref, w_ref, maps_ref, trans_ref, state_ref, diag_ref, cot_ref, send_ref
):
    blocks = grad_ref.shape[0]
    group, share, _ = trans_ref.shape
    total = jnp.zeros(cot_ref.shape, F32)
    for block in range(0, blocks, 2):
        left = jnp.concatenate([grad_ref[block], grad_ref[block + 1]], axis=1)
        total += mm_bf16(left, w_ref[:, block * WIDTH : (block + 2) * WIDTH], 1, 1)
    cot_ref[...] = total
    chips = send_ref.shape[0]
    part = WIDTH // chips
    for head in range(group):
        carried_t = mm(total[:, head * WIDTH : (head + 1) * WIDTH], maps_ref[head], 0, 0)
        high = carried_t.astype(BF16).astype(F32)
        low = carried_t - high
        state = state_ref[head].astype(F32)
        diag = diag_ref[head].astype(F32)
        trans = trans_ref[head]
        for chip in range(chips):
            mine = slice(chip * part, (chip + 1) * part)
            send_ref[chip, head, :share, :] = trans
            send_ref[chip, head, share:, :] = jnp.concatenate(
                [state[mine], diag, high[mine], low[mine]], axis=0
            ).astype(BF16)


def scan_kernel(got_ref, send_ref):
    quads, members = got_ref.shape[:2]
    share = WIDTH // members
    part = send_ref.shape[2] // 2

    def step(state, quad, dim):
        high, low = split_bf16(state)
        both = jnp.concatenate([high.astype(F32), low.astype(F32)], axis=0).astype(BF16)
        trans = jnp.concatenate(
            [got_ref[quad, member, :share, :] for member in range(members)], axis=0
        )
        rest = [got_ref[quad, member, share:, :].astype(F32) for member in range(members)]
        product = mm_bf16(both, trans, 1, dim)
        moved = product[:part] + product[part:] + state * rest[0][part : 2 * part]
        if dim == 1:
            return moved + rest[0][:part] + rest[1][:part]
        for piece in rest:
            moved = moved + (piece[2 * part : 3 * part] + piece[3 * part :])
        return moved

    ahead = jnp.zeros((part, WIDTH), F32)
    back = jnp.zeros((part, WIDTH), F32)
    for turn in range(quads):
        late = quads - 1 - turn
        for member in range(members):
            send_ref[turn, member, :part, :] = ahead
            send_ref[late, member, part:, :] = back
        if turn < quads - 1:
            ahead = step(ahead, turn, 1)
            back = step(back, late, 0)


def gather_rows(got_ref, head, which):
    chips, _, rows, _ = got_ref.shape
    part = rows // 2
    return got_ref[:, head, which * part : (which + 1) * part, :].reshape(chips * part, WIDTH)


def output_kernel(
    flags_ref, got_ref, maps_ref, other_maps_ref, grad_ref, other_grad_ref, attn_ref, send_ref
):
    group = maps_ref.shape[0] // 2
    dests, part, _ = send_ref.shape
    blocks = other_grad_ref.shape[0]
    first = flags_ref[0] * blocks
    own, other = [], []
    for head in range(group):
        state_t = gather_rows(got_ref, head, 0)
        own.append(mm(maps_ref[head], state_t, 1, 1) + maps_ref[group + head])
        other.append(mm(other_maps_ref[head], state_t, 1, 1) + other_maps_ref[group + head])
    own = jnp.concatenate(own, axis=1).astype(BF16)
    other = jnp.concatenate(other, axis=1).astype(BF16)
    attn_ref[...] = own
    left = jnp.concatenate([own, other], axis=0)
    for block in range(0, blocks, 2):
        right = jnp.concatenate(
            [
                jnp.concatenate([grad_ref[first + block], grad_ref[first + block + 1]], axis=1),
                jnp.concatenate([other_grad_ref[block], other_grad_ref[block + 1]], axis=1),
            ],
            axis=0,
        )
        term = mm_bf16(left, right, 0, 0)
        send_ref[:, :, block * WIDTH : (block + 2) * WIDTH] = term.reshape(
            dests, part, 2 * WIDTH
        ).astype(BF16)


def sum_kernel(got_ref, out_ref, *, scaling):
    chips, cores, _, width = got_ref.shape
    for core in range(cores):
        total = got_ref[0, core].astype(F32)
        for chip in range(1, chips):
            total = total + got_ref[chip, core].astype(F32)
        out_ref[:, core * width : (core + 1) * width] = total * scaling


def half_kernel(flags_ref, grad_ref, half_ref):
    blocks = half_ref.shape[0]
    half_ref[...] = grad_ref[pl.ds((1 - flags_ref[0]) * blocks, blocks)]


def carried_kernel(cot_ref, probe_ref, chip_maps_ref, carried_ref):
    group = probe_ref.shape[0]
    for head in range(group):
        cot = cot_ref[:, head * WIDTH : (head + 1) * WIDTH]
        carried_ref[head] = mm(cot, probe_ref[head], 0, 0)
        carried_ref[group + head] = mm(cot, chip_maps_ref[head], 0, 0)


def add_kernel(own_ref, other_ref, total_ref):
    group = total_ref.shape[0]
    total_ref[...] = own_ref[group:] + other_ref[group:]


def gradient_kernel(
    flags_ref, q_ref, k_ref, got_ref, other_ref, other_chip_ref, carried_ref, chip_carried_ref,
    cot_ref, tmat_ref, mix_ref, ratio_ref, uw_ref, cols_ref, q_grad_ref, k_grad_ref, v_grad_ref,
):
    length = q_ref.shape[0]
    group = tmat_ref.shape[0]
    core = flags_ref[0] == 1
    late = flags_ref[1] == 1
    q = q_ref[...].astype(F32)
    k = k_ref[...].astype(F32)
    q_inv = inverse_norm(q)
    k_inv = inverse_norm(k)
    qn = q * q_inv * WIDTH ** (-0.5)
    kn = k * k_inv
    rows, cols = ids(length)
    dq = jnp.zeros((length, WIDTH), F32)
    dk = jnp.zeros((length, WIDTH), F32)
    for head in range(group):
        span = slice(head * WIDTH, (head + 1) * WIDTH)
        state_t = gather_rows(got_ref, head, 0)
        end_t = gather_rows(got_ref, head, 1)
        for after, other, term, carried in (
            (late, other_chip_ref[head], other_chip_ref[group + head], chip_carried_ref[head]),
            (core, other_ref[head], other_ref[group + head], carried_ref[head]),
        ):
            through_state = mm(state_t, other, 1, 1) + term
            through_end = mm(end_t, other) + carried
            state_t = jnp.where(after, through_state, state_t)
            end_t = jnp.where(after, end_t, through_end)
        cot = cot_ref[:, span]
        ratio = ratio_ref[head]
        decay = cols_ref[head, 0]
        weight = cols_ref[head, 1]
        new_values = uw_ref[head, :, :WIDTH] - mm(uw_ref[head, :, WIDTH:], state_t, 1, 1)
        d_new = mm(mix_ref[head], cot, 0, 0) + mm(weight * kn, end_t, 1, 1)
        d_value = mm(tmat_ref[head], d_new, 0, 0)
        v_grad_ref[:, span] = d_value
        d_mix = mm(cot, new_values, 1, 1) * ratio
        d_gram = jnp.where(rows > cols, -mm(d_value, new_values, 1, 1) * ratio, 0.0)
        dq += decay * mm(cot, state_t) + mm(d_mix, kn)
        dk += (
            weight * mm(new_values, end_t)
            - decay * mm(d_value, state_t)
            + mm(d_mix, qn, 0, 0)
            + mm(d_gram + d_gram.T, kn)
        )
    dq = dq * WIDTH ** (-0.5)
    q_grad_ref[...] = q_inv * dq - q * (
        q_inv * q_inv * q_inv * jnp.sum(q * dq, axis=-1, keepdims=True)
    )
    k_grad_ref[...] = k_inv * dk - k * (
        k_inv * k_inv * k_inv * jnp.sum(k * dk, axis=-1, keepdims=True)
    )


def call(kernel, outs, flops, *operands):
    moved = sum(x.size * x.dtype.itemsize for x in operands) + sum(
        x.size * x.dtype.itemsize for x in outs
    )
    scalars = [x.ndim == 1 for x in operands]
    vmem = pl.BlockSpec(memory_space=pltpu.VMEM)
    smem = pl.BlockSpec(memory_space=pltpu.SMEM)
    return pl.pallas_call(
        kernel,
        out_shape=outs,
        in_specs=[smem if scalar else vmem for scalar in scalars],
        out_specs=[vmem] * len(outs),
        name=getattr(kernel, "func", kernel).__name__,
        cost_estimate=pl.CostEstimate(flops=flops, bytes_accessed=moved, transcendentals=0),
        compiler_params=pltpu.CompilerParams(vmem_limit_bytes=48 << 20),
    )(*operands)


def shape(dims, dtype=F32):
    return jax.ShapeDtypeStruct(dims, dtype)


def swap(value, axis):
    return lax.all_to_all(value, axis, 0, 0, tiled=True)


def across(value, step):
    slabs = lax.axis_size("seq")
    return lax.ppermute(value, "seq", [(slab, slab ^ step) for slab in range(slabs)])


def per_device(queries, keys, values, gate_code, beta_code, out_grad, w_out):
    length = queries.shape[0]
    group = values.shape[1] // queries.shape[1]
    slabs = lax.axis_size("seq")
    heads = lax.axis_size("head")
    chips = slabs // 2
    part = WIDTH // chips
    square = (group, length, WIDTH)
    states_shape = (2 * group, WIDTH, WIDTH)
    flat = (length, group * WIDTH)
    place = lax.axis_index("seq").astype(jnp.int32)
    flags = jnp.stack([place & 1, (place >> 1) & 1])
    full_grad = swap(jnp.broadcast_to(out_grad[None], (heads, length, WIDTH)), "head")
    pair, tmat, mix, ratio, uw, probe, local, columns = call(
        prepare_kernel,
        [
            shape(states_shape),
            shape(square),
            shape(square),
            shape(square),
            shape((group, length, 2 * WIDTH)),
            shape(square),
            shape(flat),
            shape((group, 2, length, WIDTH)),
        ],
        1 << 30,
        queries, keys, values, gate_code.T, beta_code.T,
    )
    other = across(pair, 1)
    chip, chip_maps = call(
        chip_kernel,
        [shape(states_shape), shape((2 * group, length, WIDTH))],
        1 << 28,
        flags, pair, other, probe, local,
    )
    other_chip = across(chip, 2)
    trans, state, diag, maps = call(
        quad_kernel,
        [
            shape((group, WIDTH // 4, WIDTH), BF16),
            shape((group, WIDTH, WIDTH), BF16),
            shape((group, part, WIDTH), BF16),
            shape((2 * group, length, WIDTH)),
        ],
        1 << 28,
        flags, chip, other_chip, chip_maps,
    )
    other_maps = across(maps, 1)
    cot, send = call(
        cotangent_kernel,
        [shape(flat), shape((chips, group, WIDTH // 4 + 4 * part, WIDTH), BF16)],
        1 << 28,
        full_grad, w_out, maps, trans, state, diag,
    )
    got = swap(send.reshape((slabs,) + send.shape[2:]), "seq")
    (half,) = call(
        half_kernel, [shape((heads // 2, length, WIDTH), BF16)], 1 << 20, flags, full_grad
    )
    other_half = across(half, 1)
    (own_carried,) = call(
        carried_kernel, [shape(states_shape)], 1 << 26, cot, probe, chip_maps
    )
    carried = across(own_carried, 1)
    got, carried = lax.optimization_barrier((got, carried))
    (back,) = call(
        scan_kernel,
        [shape((slabs // 4, 4, 2 * part, WIDTH))],
        1 << 27,
        got.reshape((slabs // 4, 4) + got.shape[1:]),
    )
    states = swap(back.reshape(slabs, 2 * part, WIDTH), "seq").reshape(
        chips, group, 2 * part, WIDTH
    )
    (chip_carried,) = call(add_kernel, [shape(square)], 1 << 20, own_carried, carried)
    chip_carried = across(chip_carried, 2)
    states, chip_carried = lax.optimization_barrier((states, chip_carried))
    attn_out, grad_send = call(
        output_kernel,
        [shape(flat, BF16), shape((slabs, part, heads // 2 * WIDTH), BF16)],
        1 << 28,
        flags, states, maps, other_maps, full_grad, other_half,
    )
    grad_got = swap(grad_send, "seq")
    q_grad, k_grad, v_grad = call(
        gradient_kernel,
        [shape((length, WIDTH)), shape((length, WIDTH)), shape(flat)],
        1 << 29,
        flags, queries, keys, states, other, other_chip, carried, chip_carried, cot, tmat, mix, ratio, uw, columns,
    )
    scaling = (length * slabs) ** (-0.5)
    (weight_grad,) = call(
        functools.partial(sum_kernel, scaling=scaling),
        [shape((part, heads * WIDTH))],
        1 << 20,
        grad_got.reshape((chips, 2) + grad_got.shape[1:]),
    )
    return (attn_out, q_grad, k_grad, v_grad, weight_grad)


def solution(mesh):
    in_specs = (
        P("seq", "head"),
        P("seq", "head"),
        P("seq", "head"),
        P("seq", "head"),
        P("seq", "head"),
        P("seq", "head"),
        P("head", None),
    )
    out_specs = (
        P("seq", "head"),
        P("seq", "head"),
        P("seq", "head"),
        P("seq", "head"),
        P(("head", "seq"), None),
    )
    return jax.shard_map(
        per_device, mesh=mesh, in_specs=in_specs, out_specs=out_specs, check_vma=False
    )
```

```python
import functools

import jax
import jax.numpy as jnp
from jax import lax
from jax.experimental import pallas as pl
from jax.experimental.pallas import tpu as pltpu
from jax.sharding import PartitionSpec as P

WIDTH = 128
norm_eps = 1e-06
gate_step = 1e-06
beta_steps = 256.0
F32 = jnp.float32
BF16 = jnp.bfloat16
HIGHEST = lax.Precision.HIGHEST


def mm(left, right, left_dim=1, right_dim=0):
    return lax.dot_general(
        left,
        right,
        (((left_dim,), (right_dim,)), ((), ())),
        precision=HIGHEST,
        preferred_element_type=F32,
    )


def mm_bf16(left, right, left_dim=1, right_dim=0):
    return lax.dot_general(
        left, right, (((left_dim,), (right_dim,)), ((), ())), preferred_element_type=F32
    )


def ids(length):
    rows = lax.broadcasted_iota(jnp.int32, (length, length), 0)
    cols = lax.broadcasted_iota(jnp.int32, (length, length), 1)
    return rows, cols


def unit_lower_inverse(lower, rows, cols):
    length = lower.shape[0]
    shift = 1
    pair = jnp.right_shift(rows, 1) == jnp.right_shift(cols, 1)
    inverse = jnp.where(rows == cols, 1.0, jnp.where(pair, -lower, 0.0))
    while (1 << shift) < length:
        wider = jnp.right_shift(rows, shift + 1) == jnp.right_shift(cols, shift + 1)
        inner = jnp.right_shift(rows, shift) == jnp.right_shift(cols, shift)
        off = jnp.where(wider & jnp.logical_not(inner), lower, 0.0)
        inverse = inverse - mm(inverse, mm(off, inverse))
        shift += 1
    return inverse


def inverse_norm(block):
    return lax.rsqrt(jnp.sum(block * block, axis=-1, keepdims=True) + norm_eps)


def split_bf16(value):
    high = value.astype(BF16)
    return high, (value - high.astype(F32)).astype(BF16)


def prepare_kernel(
    q_ref, k_ref, v_ref, gate_ref, beta_ref,
    pair_ref, tmat_ref, mix_ref, ratio_ref, uw_ref, probe_ref, local_ref, cols_ref,
):
    length = q_ref.shape[0]
    group = gate_ref.shape[0]
    q = q_ref[...].astype(F32)
    k = k_ref[...].astype(F32)
    qn = q * inverse_norm(q) * WIDTH ** (-0.5)
    kn = k * inverse_norm(k)
    rows, cols = ids(length)
    gram = mm(kn, kn, 1, 1)
    query_key = mm(qn, kn, 1, 1)
    tri = jnp.where(rows >= cols, 1.0, 0.0)
    logs = jnp.log1p(-(gate_ref[...].astype(F32) * gate_step))
    betas = beta_ref[...].astype(F32) / beta_steps
    for head in range(group):
        span = slice(head * WIDTH, (head + 1) * WIDTH)
        log_cum = mm(tri, jnp.broadcast_to(logs[head : head + 1, :], (length, length)), 1, 1)
        beta_row = jnp.broadcast_to(betas[head : head + 1, :], (length, length))
        ratio = jnp.exp(log_cum - log_cum.T) * beta_row
        ratio = jnp.where(rows >= cols, ratio, 0.0)
        lower = jnp.where(rows > cols, ratio * gram, 0.0)
        mix = ratio * query_key
        inverse = unit_lower_inverse(lower, rows, cols)
        decay = jnp.exp(log_cum)
        value = v_ref[:, span].astype(F32)
        uw = mm(inverse, jnp.concatenate([value, decay * kn], axis=1))
        mixed = mm(mix, uw)
        last = log_cum[length - 1 :, :]
        weight = beta_row.T * jnp.exp(last - log_cum)
        weighted = weight * kn
        uv, wk = uw[:, :WIDTH], uw[:, WIDTH:]
        pair_ref[head] = jnp.where(rows == cols, jnp.exp(last), 0.0) - mm(weighted, wk, 0, 0)
        pair_ref[group + head] = mm(uv, weighted, 0, 0)
        tmat_ref[head] = inverse
        mix_ref[head] = mix
        ratio_ref[head] = ratio
        uw_ref[head] = uw
        probe_ref[head] = decay * qn - mixed[:, WIDTH:]
        local_ref[:, span] = mixed[:, :WIDTH]
        cols_ref[head, 0] = decay
        cols_ref[head, 1] = weight


def in_order(late, own, other):
    return jnp.where(late, other, own), jnp.where(late, own, other)


def compose_heads(late, own_ref, other_ref, head, group):
    own, other = own_ref[head], other_ref[head]
    first, second = in_order(late, own, other)
    first_state, second_state = in_order(late, own_ref[group + head], other_ref[group + head])
    return mm(second, first), mm(first_state, second, 1, 1) + second_state


def compose_maps(late, other_ref, head, group, probe, local):
    moved = jnp.where(late, mm(probe, other_ref[head]), probe)
    return moved, jnp.where(late, local + mm(probe, other_ref[group + head], 1, 1), local)


def chip_kernel(flags_ref, own_ref, other_ref, probe_ref, local_ref, chip_ref, maps_ref):
    group = probe_ref.shape[0]
    late = flags_ref[0] == 1
    for head in range(group):
        span = slice(head * WIDTH, (head + 1) * WIDTH)
        chip_ref[head], chip_ref[group + head] = compose_heads(
            late, own_ref, other_ref, head, group
        )
        maps_ref[head], maps_ref[group + head] = compose_maps(
            late, other_ref, head, group, probe_ref[head], local_ref[:, span]
        )


def quad_kernel(
    flags_ref, own_ref, other_ref, chip_maps_ref, maps_ref
):
    group = chip_maps_ref.shape[0] // 2
    core = flags_ref[0] == 1
    late = flags_ref[1] == 1
    rows, cols = ids(WIDTH)
    share = WIDTH // 4
    for head in range(group):
        transition, state_t = compose_heads(late, own_ref, other_ref, head, group)
        rounded = transition.astype(BF16)
        rest = jnp.where(rows == cols, transition - rounded.astype(F32), 0.0)
        maps_ref[3 * group + head, share : 2 * share] = jnp.broadcast_to(
            jnp.sum(rest, axis=0, keepdims=True), (share, WIDTH)
        )
        quarters = [transition[at * share : (at + 1) * share] for at in range(4)]
        maps_ref[3 * group + head, :share] = jnp.where(
            late,
            jnp.where(core, quarters[3], quarters[2]),
            jnp.where(core, quarters[1], quarters[0]),
        )
        high = state_t.astype(BF16).astype(F32)
        part = jnp.where(core, state_t - high, high)
        maps_ref[2 * group + head] = jnp.where(late, 0.0, part)
        maps_ref[head], maps_ref[group + head] = compose_maps(
            late, other_ref, head, group, chip_maps_ref[head], chip_maps_ref[group + head]
        )


def cotangent_kernel(
    grad_ref, w_ref, maps_ref, cot_ref, send_ref
):
    blocks = grad_ref.shape[0]
    group = send_ref.shape[1]
    share = WIDTH // 4
    total = jnp.zeros(cot_ref.shape, F32)
    for block in range(0, blocks, 2):
        left = jnp.concatenate([grad_ref[block], grad_ref[block + 1]], axis=1)
        total += mm_bf16(left, w_ref[:, block * WIDTH : (block + 2) * WIDTH], 1, 1)
    cot_ref[...] = total
    chips = send_ref.shape[0]
    part = WIDTH // chips
    for head in range(group):
        carried_t = mm(total[:, head * WIDTH : (head + 1) * WIDTH], maps_ref[head], 0, 0)
        high = carried_t.astype(BF16).astype(F32)
        low = carried_t - high
        state = maps_ref[2 * group + head]
        diag = maps_ref[3 * group + head, share : share + part, :]
        trans = maps_ref[3 * group + head, :share, :].astype(BF16)
        for chip in range(chips):
            mine = slice(chip * part, (chip + 1) * part)
            send_ref[chip, head, :share, :] = trans
            send_ref[chip, head, share:, :] = jnp.concatenate(
                [state[mine], diag, high[mine], low[mine]], axis=0
            ).astype(BF16)


def scan_kernel(got_ref, send_ref):
    quads, members = got_ref.shape[:2]
    share = WIDTH // members
    part = send_ref.shape[2] // 2

    def step(state, quad, dim):
        high, low = split_bf16(state)
        both = jnp.concatenate([high.astype(F32), low.astype(F32)], axis=0).astype(BF16)
        trans = jnp.concatenate(
            [got_ref[quad, member, :share, :] for member in range(members)], axis=0
        )
        rest = [got_ref[quad, member, share:, :].astype(F32) for member in range(members)]
        product = mm_bf16(both, trans, 1, dim)
        moved = product[:part] + product[part:] + state * rest[0][part : 2 * part]
        if dim == 1:
            return moved + rest[0][:part] + rest[1][:part]
        for piece in rest:
            moved = moved + (piece[2 * part : 3 * part] + piece[3 * part :])
        return moved

    ahead = jnp.zeros((part, WIDTH), F32)
    back = jnp.zeros((part, WIDTH), F32)
    for turn in range(quads):
        late = quads - 1 - turn
        for member in range(members):
            send_ref[turn, member, :part, :] = ahead
            send_ref[late, member, part:, :] = back
        if turn < quads - 1:
            ahead = step(ahead, turn, 1)
            back = step(back, late, 0)


def gather_rows(got_ref, head, which):
    chips, _, rows, _ = got_ref.shape
    part = rows // 2
    return got_ref[:, head, which * part : (which + 1) * part, :].reshape(chips * part, WIDTH)


def output_kernel(
    flags_ref, got_ref, maps_ref, other_maps_ref, grad_ref, other_grad_ref, attn_ref, send_ref
):
    group = maps_ref.shape[0] // 4
    dests, part, _ = send_ref.shape
    blocks = other_grad_ref.shape[0]
    first = flags_ref[0] * blocks
    own, other = [], []
    for head in range(group):
        state_t = gather_rows(got_ref, head, 0)
        own.append(mm(maps_ref[head], state_t, 1, 1) + maps_ref[group + head])
        other.append(mm(other_maps_ref[head], state_t, 1, 1) + other_maps_ref[group + head])
    own = jnp.concatenate(own, axis=1).astype(BF16)
    other = jnp.concatenate(other, axis=1).astype(BF16)
    attn_ref[...] = own
    left = jnp.concatenate([own, other], axis=0)
    for block in range(0, blocks, 2):
        right = jnp.concatenate(
            [
                jnp.concatenate([grad_ref[first + block], grad_ref[first + block + 1]], axis=1),
                jnp.concatenate([other_grad_ref[block], other_grad_ref[block + 1]], axis=1),
            ],
            axis=0,
        )
        term = mm_bf16(left, right, 0, 0)
        send_ref[:, :, block * WIDTH : (block + 2) * WIDTH] = term.reshape(
            dests, part, 2 * WIDTH
        ).astype(BF16)


def sum_kernel(got_ref, out_ref, *, scaling):
    chips, cores, _, width = got_ref.shape
    for core in range(cores):
        total = got_ref[0, core].astype(F32)
        for chip in range(1, chips):
            total = total + got_ref[chip, core].astype(F32)
        out_ref[:, core * width : (core + 1) * width] = total * scaling


def half_kernel(flags_ref, grad_ref, half_ref):
    blocks = half_ref.shape[0]
    half_ref[...] = grad_ref[pl.ds((1 - flags_ref[0]) * blocks, blocks)]


def sibling_kernel(
    maps_ref, cot_ref, probe_ref, chip_maps_ref, pack_ref, term_ref
):
    group = probe_ref.shape[0]
    pack_ref[: 2 * group] = maps_ref[: 2 * group]
    for head in range(group):
        cot = cot_ref[:, head * WIDTH : (head + 1) * WIDTH]
        pack_ref[2 * group + head] = mm(cot, probe_ref[head], 0, 0)
        term_ref[head] = mm(cot, chip_maps_ref[head], 0, 0)


def gradient_kernel(
    flags_ref, q_ref, k_ref, got_ref, other_ref, other_chip_ref, other_pack_ref, near_ref, far_ref,
    cot_ref, tmat_ref, mix_ref, ratio_ref, uw_ref, cols_ref, q_grad_ref, k_grad_ref, v_grad_ref,
):
    length = q_ref.shape[0]
    group = tmat_ref.shape[0]
    core = flags_ref[0] == 1
    late = flags_ref[1] == 1
    q = q_ref[...].astype(F32)
    k = k_ref[...].astype(F32)
    q_inv = inverse_norm(q)
    k_inv = inverse_norm(k)
    qn = q * q_inv * WIDTH ** (-0.5)
    kn = k * k_inv
    rows, cols = ids(length)
    dq = jnp.zeros((length, WIDTH), F32)
    dk = jnp.zeros((length, WIDTH), F32)
    for head in range(group):
        span = slice(head * WIDTH, (head + 1) * WIDTH)
        state_t = gather_rows(got_ref, head, 0)
        end_t = gather_rows(got_ref, head, 1)
        for after, other, term, carried in (
            (late, other_chip_ref[head], other_chip_ref[group + head], near_ref[head] + far_ref[head]),
            (core, other_ref[head], other_ref[group + head], other_pack_ref[2 * group + head]),
        ):
            through_state = mm(state_t, other, 1, 1) + term
            through_end = mm(end_t, other) + carried
            state_t = jnp.where(after, through_state, state_t)
            end_t = jnp.where(after, end_t, through_end)
        cot = cot_ref[:, span]
        ratio = ratio_ref[head]
        decay = cols_ref[head, 0]
        weight = cols_ref[head, 1]
        new_values = uw_ref[head, :, :WIDTH] - mm(uw_ref[head, :, WIDTH:], state_t, 1, 1)
        d_new = mm(mix_ref[head], cot, 0, 0) + mm(weight * kn, end_t, 1, 1)
        d_value = mm(tmat_ref[head], d_new, 0, 0)
        v_grad_ref[:, span] = d_value
        d_mix = mm(cot, new_values, 1, 1) * ratio
        d_gram = jnp.where(rows > cols, -mm(d_value, new_values, 1, 1) * ratio, 0.0)
        dq += decay * mm(cot, state_t) + mm(d_mix, kn)
        dk += (
            weight * mm(new_values, end_t)
            - decay * mm(d_value, state_t)
            + mm(d_mix, qn, 0, 0)
            + mm(d_gram + d_gram.T, kn)
        )
    dq = dq * WIDTH ** (-0.5)
    q_grad_ref[...] = q_inv * dq - q * (
        q_inv * q_inv * q_inv * jnp.sum(q * dq, axis=-1, keepdims=True)
    )
    k_grad_ref[...] = k_inv * dk - k * (
        k_inv * k_inv * k_inv * jnp.sum(k * dk, axis=-1, keepdims=True)
    )


def call(kernel, outs, flops, *operands):
    moved = sum(x.size * x.dtype.itemsize for x in operands) + sum(
        x.size * x.dtype.itemsize for x in outs
    )
    scalars = [x.ndim == 1 for x in operands]
    vmem = pl.BlockSpec(memory_space=pltpu.VMEM)
    smem = pl.BlockSpec(memory_space=pltpu.SMEM)
    return pl.pallas_call(
        kernel,
        out_shape=outs,
        in_specs=[smem if scalar else vmem for scalar in scalars],
        out_specs=[vmem] * len(outs),
        name=getattr(kernel, "func", kernel).__name__,
        cost_estimate=pl.CostEstimate(flops=flops, bytes_accessed=moved, transcendentals=0),
        compiler_params=pltpu.CompilerParams(vmem_limit_bytes=48 << 20),
    )(*operands)


def shape(dims, dtype=F32):
    return jax.ShapeDtypeStruct(dims, dtype)


def swap(value, axis):
    return lax.all_to_all(value, axis, 0, 0, tiled=True)


def across(value, step):
    slabs = lax.axis_size("seq")
    return lax.ppermute(value, "seq", [(slab, slab ^ step) for slab in range(slabs)])


def per_device(queries, keys, values, gate_code, beta_code, out_grad, w_out):
    length = queries.shape[0]
    group = values.shape[1] // queries.shape[1]
    slabs = lax.axis_size("seq")
    heads = lax.axis_size("head")
    chips = slabs // 2
    part = WIDTH // chips
    square = (group, length, WIDTH)
    states_shape = (2 * group, WIDTH, WIDTH)
    flat = (length, group * WIDTH)
    place = lax.axis_index("seq").astype(jnp.int32)
    flags = jnp.stack([place & 1, (place >> 1) & 1])
    full_grad = swap(jnp.broadcast_to(out_grad[None], (heads, length, WIDTH)), "head")
    pair, tmat, mix, ratio, uw, probe, local, columns = call(
        prepare_kernel,
        [
            shape(states_shape),
            shape(square),
            shape(square),
            shape(square),
            shape((group, length, 2 * WIDTH)),
            shape(square),
            shape(flat),
            shape((group, 2, length, WIDTH)),
        ],
        1 << 30,
        queries, keys, values, gate_code.T, beta_code.T,
    )
    other = across(pair, 1)
    chip, chip_maps = call(
        chip_kernel,
        [shape(states_shape), shape((2 * group, length, WIDTH))],
        1 << 28,
        flags, pair, other, probe, local,
    )
    other_chip = across(chip, 2)
    (maps,) = call(
        quad_kernel,
        [shape((4 * group, WIDTH, WIDTH))],
        1 << 28,
        flags, chip, other_chip, chip_maps,
    )
    cot, send = call(
        cotangent_kernel,
        [shape(flat), shape((chips, group, WIDTH // 4 + 4 * part, WIDTH), BF16)],
        1 << 28,
        full_grad, w_out, maps,
    )
    got = swap(send.reshape((slabs,) + send.shape[2:]), "seq")
    pack, term = call(
        sibling_kernel,
        [shape((3 * group, length, WIDTH)), shape(square)],
        1 << 26,
        maps, cot, probe, chip_maps,
    )
    near_term = across(term, 2)
    other_pack = across(pack, 1)
    (back,) = call(
        scan_kernel,
        [shape((slabs // 4, 4, 2 * part, WIDTH))],
        1 << 27,
        got.reshape((slabs // 4, 4) + got.shape[1:]),
    )
    back, near_term = lax.optimization_barrier((back, near_term))
    far_term = across(near_term, 1)
    (half,) = call(
        half_kernel, [shape((heads // 2, length, WIDTH), BF16)], 1 << 20, flags, full_grad
    )
    other_half = across(half, 1)
    states = swap(back.reshape(slabs, 2 * part, WIDTH), "seq").reshape(
        chips, group, 2 * part, WIDTH
    )
    attn_out, grad_send = call(
        output_kernel,
        [shape(flat, BF16), shape((slabs, part, heads // 2 * WIDTH), BF16)],
        1 << 28,
        flags, states, maps, other_pack, full_grad, other_half,
    )
    grad_got = swap(grad_send, "seq")
    q_grad, k_grad, v_grad = call(
        gradient_kernel,
        [shape((length, WIDTH)), shape((length, WIDTH)), shape(flat)],
        1 << 29,
        flags, queries, keys, states, other, other_chip, other_pack, near_term, far_term, cot, tmat, mix, ratio, uw, columns,
    )
    scaling = (length * slabs) ** (-0.5)
    (weight_grad,) = call(
        functools.partial(sum_kernel, scaling=scaling),
        [shape((part, heads * WIDTH))],
        1 << 20,
        grad_got.reshape((chips, 2) + grad_got.shape[1:]),
    )
    return (attn_out, q_grad, k_grad, v_grad, weight_grad)


def solution(mesh):
    in_specs = (
        P("seq", "head"),
        P("seq", "head"),
        P("seq", "head"),
        P("seq", "head"),
        P("seq", "head"),
        P("seq", "head"),
        P("head", None),
    )
    out_specs = (
        P("seq", "head"),
        P("seq", "head"),
        P("seq", "head"),
        P("seq", "head"),
        P(("head", "seq"), None),
    )
    return jax.shard_map(
        per_device, mesh=mesh, in_specs=in_specs, out_specs=out_specs, check_vma=False
    )
```

```python
import functools

import jax
import jax.numpy as jnp
from jax import lax
from jax.experimental import pallas as pl
from jax.experimental.pallas import tpu as pltpu
from jax.sharding import PartitionSpec as P

WIDTH = 128
norm_eps = 1e-06
gate_step = 1e-06
beta_steps = 256.0
F32 = jnp.float32
BF16 = jnp.bfloat16
HIGHEST = lax.Precision.HIGHEST


def mm(left, right, left_dim=1, right_dim=0):
    return lax.dot_general(
        left,
        right,
        (((left_dim,), (right_dim,)), ((), ())),
        precision=HIGHEST,
        preferred_element_type=F32,
    )


def mm_bf16(left, right, left_dim=1, right_dim=0):
    return lax.dot_general(
        left, right, (((left_dim,), (right_dim,)), ((), ())), preferred_element_type=F32
    )


def ids(length):
    rows = lax.broadcasted_iota(jnp.int32, (length, length), 0)
    cols = lax.broadcasted_iota(jnp.int32, (length, length), 1)
    return rows, cols


def unit_lower_inverse(lower, rows, cols):
    length = lower.shape[0]
    shift = 1
    pair = jnp.right_shift(rows, 1) == jnp.right_shift(cols, 1)
    inverse = jnp.where(rows == cols, 1.0, jnp.where(pair, -lower, 0.0))
    while (1 << shift) < length:
        wider = jnp.right_shift(rows, shift + 1) == jnp.right_shift(cols, shift + 1)
        inner = jnp.right_shift(rows, shift) == jnp.right_shift(cols, shift)
        off = jnp.where(wider & jnp.logical_not(inner), lower, 0.0)
        inverse = inverse - mm(inverse, mm(off, inverse))
        shift += 1
    return inverse


def inverse_norm(block):
    return lax.rsqrt(jnp.sum(block * block, axis=-1, keepdims=True) + norm_eps)


def split_bf16(value):
    high = value.astype(BF16)
    return high, (value - high.astype(F32)).astype(BF16)


def prepare_kernel(
    q_ref, k_ref, v_ref, gate_ref, beta_ref,
    pair_ref, tmat_ref, mix_ref, ratio_ref, uw_ref, probe_ref, local_ref, cols_ref,
):
    length = q_ref.shape[0]
    group = gate_ref.shape[0]
    q = q_ref[...].astype(F32)
    k = k_ref[...].astype(F32)
    qn = q * inverse_norm(q) * WIDTH ** (-0.5)
    kn = k * inverse_norm(k)
    rows, cols = ids(length)
    gram = mm(kn, kn, 1, 1)
    query_key = mm(qn, kn, 1, 1)
    tri = jnp.where(rows >= cols, 1.0, 0.0)
    logs = jnp.log1p(-(gate_ref[...].astype(F32) * gate_step))
    betas = beta_ref[...].astype(F32) / beta_steps
    for head in range(group):
        span = slice(head * WIDTH, (head + 1) * WIDTH)
        log_cum = mm(tri, jnp.broadcast_to(logs[head : head + 1, :], (length, length)), 1, 1)
        beta_row = jnp.broadcast_to(betas[head : head + 1, :], (length, length))
        ratio = jnp.exp(log_cum - log_cum.T) * beta_row
        ratio = jnp.where(rows >= cols, ratio, 0.0)
        lower = jnp.where(rows > cols, ratio * gram, 0.0)
        mix = ratio * query_key
        inverse = unit_lower_inverse(lower, rows, cols)
        decay = jnp.exp(log_cum)
        value = v_ref[:, span].astype(F32)
        uw = mm(inverse, jnp.concatenate([value, decay * kn], axis=1))
        mixed = mm(mix, uw)
        last = log_cum[length - 1 :, :]
        weight = beta_row.T * jnp.exp(last - log_cum)
        weighted = weight * kn
        uv, wk = uw[:, :WIDTH], uw[:, WIDTH:]
        pair_ref[head] = jnp.where(rows == cols, jnp.exp(last), 0.0) - mm(weighted, wk, 0, 0)
        pair_ref[group + head] = mm(uv, weighted, 0, 0)
        tmat_ref[head] = inverse
        mix_ref[head] = mix
        ratio_ref[head] = ratio
        uw_ref[head] = uw
        probe_ref[head] = decay * qn - mixed[:, WIDTH:]
        local_ref[:, span] = mixed[:, :WIDTH]
        cols_ref[head, 0] = decay
        cols_ref[head, 1] = weight


def in_order(late, own, other):
    return jnp.where(late, other, own), jnp.where(late, own, other)


def compose_heads(late, own_ref, other_ref, head, group):
    own, other = own_ref[head], other_ref[head]
    first, second = in_order(late, own, other)
    first_state, second_state = in_order(late, own_ref[group + head], other_ref[group + head])
    return mm(second, first), mm(first_state, second, 1, 1) + second_state


def compose_maps(late, other_ref, head, group, probe, local):
    moved = jnp.where(late, mm(probe, other_ref[head]), probe)
    return moved, jnp.where(late, local + mm(probe, other_ref[group + head], 1, 1), local)


def chip_kernel(flags_ref, own_ref, other_ref, probe_ref, local_ref, chip_ref, maps_ref):
    group = probe_ref.shape[0]
    late = flags_ref[0] == 1
    for head in range(group):
        span = slice(head * WIDTH, (head + 1) * WIDTH)
        chip_ref[head], chip_ref[group + head] = compose_heads(
            late, own_ref, other_ref, head, group
        )
        maps_ref[head], maps_ref[group + head] = compose_maps(
            late, other_ref, head, group, probe_ref[head], local_ref[:, span]
        )


def quad_kernel(
    flags_ref, own_ref, other_ref, chip_maps_ref, maps_ref
):
    group = chip_maps_ref.shape[0] // 2
    core = flags_ref[0] == 1
    late = flags_ref[1] == 1
    rows, cols = ids(WIDTH)
    share = WIDTH // 4
    for head in range(group):
        transition, state_t = compose_heads(late, own_ref, other_ref, head, group)
        rounded = transition.astype(BF16)
        rest = jnp.where(rows == cols, transition - rounded.astype(F32), 0.0)
        diag = jnp.broadcast_to(jnp.sum(rest, axis=0, keepdims=True), (WIDTH, WIDTH))
        quarters = [transition[at * share : (at + 1) * share] for at in range(4)]
        maps_ref[3 * group + head, :share] = jnp.where(
            late,
            jnp.where(core, quarters[3], quarters[2]),
            jnp.where(core, quarters[1], quarters[0]),
        )
        high = state_t.astype(BF16).astype(F32)
        part = jnp.where(core, state_t - high, high)
        maps_ref[2 * group + head] = jnp.where(late, diag, part)
        maps_ref[head], maps_ref[group + head] = compose_maps(
            late, other_ref, head, group, chip_maps_ref[head], chip_maps_ref[group + head]
        )


def cotangent_kernel(
    grad_ref, w_ref, maps_ref, cot_ref, send_ref
):
    blocks = grad_ref.shape[0]
    group = send_ref.shape[1]
    share = WIDTH // 4
    total = jnp.zeros(cot_ref.shape, F32)
    for block in range(0, blocks, 2):
        left = jnp.concatenate([grad_ref[block], grad_ref[block + 1]], axis=1)
        total += mm_bf16(left, w_ref[:, block * WIDTH : (block + 2) * WIDTH], 1, 1)
    cot_ref[...] = total
    chips = send_ref.shape[0]
    part = WIDTH // chips
    for head in range(group):
        carried_t = mm(total[:, head * WIDTH : (head + 1) * WIDTH], maps_ref[head], 0, 0)
        high = carried_t.astype(BF16).astype(F32)
        low = carried_t - high
        state = maps_ref[2 * group + head]
        trans = maps_ref[3 * group + head, :share, :].astype(BF16)
        for chip in range(chips):
            mine = slice(chip * part, (chip + 1) * part)
            send_ref[chip, head, :share, :] = trans
            send_ref[chip, head, share:, :] = jnp.concatenate(
                [state[mine], high[mine], low[mine]], axis=0
            ).astype(BF16)


def scan_kernel(got_ref, send_ref):
    quads, members = got_ref.shape[:2]
    share = WIDTH // members
    part = send_ref.shape[2] // 2

    def step(state, quad, dim):
        high, low = split_bf16(state)
        both = jnp.concatenate([high.astype(F32), low.astype(F32)], axis=0).astype(BF16)
        trans = jnp.concatenate(
            [got_ref[quad, member, :share, :] for member in range(members)], axis=0
        )
        rest = [got_ref[quad, member, share:, :].astype(F32) for member in range(members)]
        product = mm_bf16(both, trans, 1, dim)
        moved = product[:part] + product[part:] + state * rest[2][:part]
        if dim == 1:
            return moved + rest[0][:part] + rest[1][:part]
        for piece in rest:
            moved = moved + (piece[part : 2 * part] + piece[2 * part :])
        return moved

    ahead = jnp.zeros((part, WIDTH), F32)
    back = jnp.zeros((part, WIDTH), F32)
    for turn in range(quads):
        late = quads - 1 - turn
        for member in range(members):
            send_ref[turn, member, :part, :] = ahead
            send_ref[late, member, part:, :] = back
        if turn < quads - 1:
            ahead = step(ahead, turn, 1)
            back = step(back, late, 0)


def gather_rows(got_ref, head, which):
    chips, _, rows, _ = got_ref.shape
    part = rows // 2
    return got_ref[:, head, which * part : (which + 1) * part, :].reshape(chips * part, WIDTH)


def output_kernel(
    flags_ref, got_ref, maps_ref, other_maps_ref, grad_ref, other_grad_ref, attn_ref, send_ref
):
    group = maps_ref.shape[0] // 4
    dests, part, _ = send_ref.shape
    blocks = other_grad_ref.shape[0]
    first = flags_ref[0] * blocks
    own, other = [], []
    for head in range(group):
        state_t = gather_rows(got_ref, head, 0)
        own.append(mm(maps_ref[head], state_t, 1, 1) + maps_ref[group + head])
        other.append(mm(other_maps_ref[head], state_t, 1, 1) + other_maps_ref[group + head])
    own = jnp.concatenate(own, axis=1).astype(BF16)
    other = jnp.concatenate(other, axis=1).astype(BF16)
    attn_ref[...] = own
    left = jnp.concatenate([own, other], axis=0)
    for block in range(0, blocks, 2):
        right = jnp.concatenate(
            [
                jnp.concatenate([grad_ref[first + block], grad_ref[first + block + 1]], axis=1),
                jnp.concatenate([other_grad_ref[block], other_grad_ref[block + 1]], axis=1),
            ],
            axis=0,
        )
        term = mm_bf16(left, right, 0, 0)
        send_ref[:, :, block * WIDTH : (block + 2) * WIDTH] = term.reshape(
            dests, part, 2 * WIDTH
        ).astype(BF16)


def sum_kernel(got_ref, out_ref, *, scaling):
    chips, cores, _, width = got_ref.shape
    for core in range(cores):
        total = got_ref[0, core].astype(F32)
        for chip in range(1, chips):
            total = total + got_ref[chip, core].astype(F32)
        out_ref[:, core * width : (core + 1) * width] = total * scaling


def half_kernel(flags_ref, grad_ref, half_ref):
    blocks = half_ref.shape[0]
    half_ref[...] = grad_ref[pl.ds((1 - flags_ref[0]) * blocks, blocks)]


def sibling_kernel(
    maps_ref, cot_ref, probe_ref, chip_maps_ref, pack_ref, term_ref
):
    group = probe_ref.shape[0]
    pack_ref[: 2 * group] = maps_ref[: 2 * group]
    for head in range(group):
        cot = cot_ref[:, head * WIDTH : (head + 1) * WIDTH]
        pack_ref[2 * group + head] = mm(cot, probe_ref[head], 0, 0)
        term_ref[head] = mm(cot, chip_maps_ref[head], 0, 0)


def gradient_kernel(
    flags_ref, q_ref, k_ref, got_ref, other_ref, other_chip_ref, other_pack_ref, near_ref, far_ref,
    cot_ref, tmat_ref, mix_ref, ratio_ref, uw_ref, cols_ref, q_grad_ref, k_grad_ref, v_grad_ref,
):
    length = q_ref.shape[0]
    group = tmat_ref.shape[0]
    core = flags_ref[0] == 1
    late = flags_ref[1] == 1
    q = q_ref[...].astype(F32)
    k = k_ref[...].astype(F32)
    q_inv = inverse_norm(q)
    k_inv = inverse_norm(k)
    qn = q * q_inv * WIDTH ** (-0.5)
    kn = k * k_inv
    rows, cols = ids(length)
    dq = jnp.zeros((length, WIDTH), F32)
    dk = jnp.zeros((length, WIDTH), F32)
    for head in range(group):
        span = slice(head * WIDTH, (head + 1) * WIDTH)
        state_t = gather_rows(got_ref, head, 0)
        end_t = gather_rows(got_ref, head, 1)
        for after, other, term, carried in (
            (late, other_chip_ref[head], other_chip_ref[group + head], near_ref[head] + far_ref[head]),
            (core, other_ref[head], other_ref[group + head], other_pack_ref[2 * group + head]),
        ):
            through_state = mm(state_t, other, 1, 1) + term
            through_end = mm(end_t, other) + carried
            state_t = jnp.where(after, through_state, state_t)
            end_t = jnp.where(after, end_t, through_end)
        cot = cot_ref[:, span]
        ratio = ratio_ref[head]
        decay = cols_ref[head, 0]
        weight = cols_ref[head, 1]
        new_values = uw_ref[head, :, :WIDTH] - mm(uw_ref[head, :, WIDTH:], state_t, 1, 1)
        d_new = mm(mix_ref[head], cot, 0, 0) + mm(weight * kn, end_t, 1, 1)
        d_value = mm(tmat_ref[head], d_new, 0, 0)
        v_grad_ref[:, span] = d_value
        d_mix = mm(cot, new_values, 1, 1) * ratio
        d_gram = jnp.where(rows > cols, -mm(d_value, new_values, 1, 1) * ratio, 0.0)
        dq += decay * mm(cot, state_t) + mm(d_mix, kn)
        dk += (
            weight * mm(new_values, end_t)
            - decay * mm(d_value, state_t)
            + mm(d_mix, qn, 0, 0)
            + mm(d_gram + d_gram.T, kn)
        )
    dq = dq * WIDTH ** (-0.5)
    q_grad_ref[...] = q_inv * dq - q * (
        q_inv * q_inv * q_inv * jnp.sum(q * dq, axis=-1, keepdims=True)
    )
    k_grad_ref[...] = k_inv * dk - k * (
        k_inv * k_inv * k_inv * jnp.sum(k * dk, axis=-1, keepdims=True)
    )


def call(kernel, outs, flops, *operands):
    moved = sum(x.size * x.dtype.itemsize for x in operands) + sum(
        x.size * x.dtype.itemsize for x in outs
    )
    scalars = [x.ndim == 1 for x in operands]
    vmem = pl.BlockSpec(memory_space=pltpu.VMEM)
    smem = pl.BlockSpec(memory_space=pltpu.SMEM)
    return pl.pallas_call(
        kernel,
        out_shape=outs,
        in_specs=[smem if scalar else vmem for scalar in scalars],
        out_specs=[vmem] * len(outs),
        name=getattr(kernel, "func", kernel).__name__,
        cost_estimate=pl.CostEstimate(flops=flops, bytes_accessed=moved, transcendentals=0),
        compiler_params=pltpu.CompilerParams(vmem_limit_bytes=48 << 20),
    )(*operands)


def shape(dims, dtype=F32):
    return jax.ShapeDtypeStruct(dims, dtype)


def swap(value, axis):
    return lax.all_to_all(value, axis, 0, 0, tiled=True)


def across(value, step):
    slabs = lax.axis_size("seq")
    return lax.ppermute(value, "seq", [(slab, slab ^ step) for slab in range(slabs)])


def per_device(queries, keys, values, gate_code, beta_code, out_grad, w_out):
    length = queries.shape[0]
    group = values.shape[1] // queries.shape[1]
    slabs = lax.axis_size("seq")
    heads = lax.axis_size("head")
    chips = slabs // 2
    part = WIDTH // chips
    square = (group, length, WIDTH)
    states_shape = (2 * group, WIDTH, WIDTH)
    flat = (length, group * WIDTH)
    place = lax.axis_index("seq").astype(jnp.int32)
    flags = jnp.stack([place & 1, (place >> 1) & 1])
    full_grad = swap(jnp.broadcast_to(out_grad[None], (heads, length, WIDTH)), "head")
    pair, tmat, mix, ratio, uw, probe, local, columns = call(
        prepare_kernel,
        [
            shape(states_shape),
            shape(square),
            shape(square),
            shape(square),
            shape((group, length, 2 * WIDTH)),
            shape(square),
            shape(flat),
            shape((group, 2, length, WIDTH)),
        ],
        1 << 30,
        queries, keys, values, gate_code.T, beta_code.T,
    )
    other = across(pair, 1)
    chip, chip_maps = call(
        chip_kernel,
        [shape(states_shape), shape((2 * group, length, WIDTH))],
        1 << 28,
        flags, pair, other, probe, local,
    )
    other_chip = across(chip, 2)
    (maps,) = call(
        quad_kernel,
        [shape((4 * group, WIDTH, WIDTH))],
        1 << 28,
        flags, chip, other_chip, chip_maps,
    )
    cot, send = call(
        cotangent_kernel,
        [shape(flat), shape((chips, group, WIDTH // 4 + 3 * part, WIDTH), BF16)],
        1 << 28,
        full_grad, w_out, maps,
    )
    got = swap(send.reshape((slabs,) + send.shape[2:]), "seq")
    pack, term = call(
        sibling_kernel,
        [shape((3 * group, length, WIDTH)), shape(square)],
        1 << 26,
        maps, cot, probe, chip_maps,
    )
    near_term = across(term, 2)
    other_pack = across(pack, 1)
    (back,) = call(
        scan_kernel,
        [shape((slabs // 4, 4, 2 * part, WIDTH))],
        1 << 27,
        got.reshape((slabs // 4, 4) + got.shape[1:]),
    )
    back, near_term = lax.optimization_barrier((back, near_term))
    far_term = across(near_term, 1)
    (half,) = call(
        half_kernel, [shape((heads // 2, length, WIDTH), BF16)], 1 << 20, flags, full_grad
    )
    other_half = across(half, 1)
    states = swap(back.reshape(slabs, 2 * part, WIDTH), "seq").reshape(
        chips, group, 2 * part, WIDTH
    )
    attn_out, grad_send = call(
        output_kernel,
        [shape(flat, BF16), shape((slabs, part, heads // 2 * WIDTH), BF16)],
        1 << 28,
        flags, states, maps, other_pack, full_grad, other_half,
    )
    grad_got = swap(grad_send, "seq")
    q_grad, k_grad, v_grad = call(
        gradient_kernel,
        [shape((length, WIDTH)), shape((length, WIDTH)), shape(flat)],
        1 << 29,
        flags, queries, keys, states, other, other_chip, other_pack, near_term, far_term, cot, tmat, mix, ratio, uw, columns,
    )
    scaling = (length * slabs) ** (-0.5)
    (weight_grad,) = call(
        functools.partial(sum_kernel, scaling=scaling),
        [shape((part, heads * WIDTH))],
        1 << 20,
        grad_got.reshape((chips, 2) + grad_got.shape[1:]),
    )
    return (attn_out, q_grad, k_grad, v_grad, weight_grad)


def solution(mesh):
    in_specs = (
        P("seq", "head"),
        P("seq", "head"),
        P("seq", "head"),
        P("seq", "head"),
        P("seq", "head"),
        P("seq", "head"),
        P("head", None),
    )
    out_specs = (
        P("seq", "head"),
        P("seq", "head"),
        P("seq", "head"),
        P("seq", "head"),
        P(("head", "seq"), None),
    )
    return jax.shard_map(
        per_device, mesh=mesh, in_specs=in_specs, out_specs=out_specs, check_vma=False
    )
```
